32 devices in a mesh: sector: 16 (over z, x, core), radial: 2 (over y).
Axes of the slice: x: 2, y: 2, z: 4, core: 2. Of those that a mesh axis runs over, the one named last changes fastest.
Arguments:
- loads: bfloat16 [32, 1536, 256], P('sector', 'radial'), may hold values from -6 to 6
- state: bfloat16 [32, 1536, 256], P('sector', 'radial'), may hold values from -0.375 to 0.375
- factors: bfloat16 [16, 2, 1536, 1024], P('sector', None, 'radial')
- assign: int32 [16], replicated, may hold values from 0 to 15, each once
- iface: int32 [2, 2, 128], P('radial'), may hold values from 0 to 767, as said below
Outputs:
- sensitivity: float32 [32, 1536], P('sector', 'radial')
The draws below stay inside these ranges and needn't reach their ends.
Inputs may be any that keep to these rules, and one draw needn't show every extreme that they name: `assign`: each slot holds a different harmonic; the value 0 stands for the slot that holds harmonics 0 and 16, any other value h for harmonic h. `iface`: within one cycle the 256 listed positions are all different.
All inputs are finite; a program needn't handle non-finite values.
Results may differ from the reference program's by a relative error of at most 0.013.
Values may be sent and summed in bfloat16 or wider, within the bound.
No kernel may reach another device: no remote copies, remote signals or barrier semaphores. Data moves between devices by JAX's collectives and lax.ppermute only.
A program may use at most 128 MiB of HBM per device.

```python
import math
import jax
import jax.numpy as jnp
from jax import lax

DOF_CYCLE = 768
FACE = 128
SECTORS = 32
SLOTS = 16
CYCLES = 2
DOFS = 1536
RHS = 256


def draw_iface(key, part):
    cycle_keys = jax.random.split(key, CYCLES)

    def one_cycle(cycle_key):
        first_key, second_key = jax.random.split(cycle_key)
        middle = jax.random.permutation(first_key, jnp.arange(1, DOF_CYCLE - 1, dtype=jnp.int32))
        corners = jnp.array([0, DOF_CYCLE - 1], dtype=jnp.int32)
        chosen = jnp.concatenate([corners, middle[:2 * FACE - 2]])
        chosen = jax.random.permutation(second_key, chosen)
        return chosen.reshape(2, FACE)
    return jax.vmap(one_cycle)(cycle_keys)


def draw_factors(key, part):
    width = DOF_CYCLE + 2 * FACE
    base_scale = (2.0 * (DOF_CYCLE + 18.0 * FACE)) ** (-0.5)
    column = jnp.arange(width, dtype=jnp.int32)
    column_scale = jnp.where(column < DOF_CYCLE, 1.0, 3.0).astype(jnp.float32) * base_scale
    value_key = jax.random.fold_in(key, 11)
    values = jnp.clip(jax.random.normal(value_key, (SLOTS, 2, DOFS, width), jnp.float32), -4.0, 4.0)
    return (values * column_scale[None, None, None, :]).astype(jnp.bfloat16)


def shard_levels(rng, extent, pieces, low, top_value):
    loudness, own = 1.0, jax.random.fold_in(rng, 6)
    for dim, blocks in pieces:
        heights = jnp.exp(jax.random.uniform(jax.random.fold_in(own, dim), (blocks,), jnp.float32, low / len(pieces), top_value / len(pieces)))
        loudness = loudness * jnp.repeat(heights, extent[dim] // blocks).reshape([-1 if axis == dim else 1 for axis in range(len(extent))])
    return loudness


def bell_draw(stream_key, dims, spread, most, pieces=(), kind=jnp.bfloat16):
    values = jax.random.normal(stream_key, dims, jnp.float32) * spread
    if len(pieces) > 0:
        values = shard_levels(stream_key, dims, pieces, -0.22, 0.18) * values
    return jnp.clip(values, min=-most, max=most).astype(kind)


def setup_inputs(seed: int = 0) -> dict:
    arg_keys = jax.random.split(jax.random.key(seed), 6)
    return {
        "loads": bell_draw(arg_keys[0], (SECTORS, DOFS, RHS), 1.0, 6.0, ((0, 16), (1, 2))),
        "state": bell_draw(arg_keys[1], (SECTORS, DOFS, RHS), RHS ** -0.5, 0.375, ((0, 16), (1, 2))),
        "factors": draw_factors(jax.random.fold_in(arg_keys[5], 71), 0),
        "assign": jax.random.permutation(arg_keys[3], SLOTS).astype(jnp.int32),
        "iface": draw_iface(jax.random.fold_in(arg_keys[5], 71), 0),
    }


def forward_table(assign, sectors):
    harmonic = assign.astype(jnp.int32)
    position = jnp.arange(sectors, dtype=jnp.int32)
    phases = (harmonic[:, None] * position[None, :]) % sectors
    angles = phases.astype(jnp.float32) * (2.0 * math.pi / sectors)
    paired = (harmonic == 0)[:, None]
    alternate = (1 - 2 * (position % 2)).astype(jnp.float32)[None, :]
    real_rows = jnp.cos(angles)
    imag_rows = jnp.where(paired, alternate, -jnp.sin(angles))
    stacked = jnp.stack([real_rows, imag_rows], axis=1)
    return stacked.reshape(2 * harmonic.shape[0], sectors).astype(jnp.bfloat16)


def inverse_table(assign, sectors):
    harmonic = assign.astype(jnp.int32)
    position = jnp.arange(sectors, dtype=jnp.int32)
    phases = (harmonic[:, None] * position[None, :]) % sectors
    angles = phases.astype(jnp.float32) * (2.0 * math.pi / sectors)
    paired = (harmonic == 0)[:, None]
    alternate = (1 - 2 * (position % 2)).astype(jnp.float32)[None, :]
    real_cols = jnp.where(paired, 1.0, 2.0) * jnp.cos(angles) / sectors
    imag_cols = jnp.where(paired, alternate, -2.0 * jnp.sin(angles)) / sectors
    stacked = jnp.stack([real_cols, imag_cols], axis=1)
    return jnp.transpose(stacked.reshape(2 * harmonic.shape[0], sectors)).astype(jnp.bfloat16)


def transposed(weight, operand):
    return lax.dot_general(weight, operand, (((0,), (0,)), ((), ())), preferred_element_type=jnp.float32)


def solve_slot(spectrum, weight_real, weight_imag, paired):
    real_real = jnp.dot(weight_real, spectrum[0], preferred_element_type=jnp.float32)
    imag_imag = jnp.dot(weight_imag, spectrum[1], preferred_element_type=jnp.float32)
    imag_real = jnp.dot(weight_imag, spectrum[0], preferred_element_type=jnp.float32)
    real_imag = jnp.dot(weight_real, spectrum[1], preferred_element_type=jnp.float32)
    middle_real = jnp.where(paired, real_real, real_real - imag_imag)
    middle_imag = jnp.where(paired, imag_imag, imag_real + real_imag)
    middle = jnp.stack([middle_real, middle_imag]).astype(jnp.bfloat16)
    back_real = transposed(weight_real, middle[0])
    back_imag = transposed(weight_imag, middle[1])
    cross_real = transposed(weight_real, middle[1])
    cross_imag = transposed(weight_imag, middle[0])
    final_real = jnp.where(paired, back_real, back_real + back_imag)
    final_imag = jnp.where(paired, back_imag, cross_real - cross_imag)
    return jnp.stack([final_real, final_imag])


def reference(loads, state, factors, assign, iface):
    forward = forward_table(assign, SECTORS)
    inverse = inverse_table(assign, SECTORS)

    def assemble_cycle(cycle_index):
        offset = cycle_index * DOF_CYCLE
        cycle_block = lax.dynamic_slice_in_dim(loads, offset, DOF_CYCLE, 1)
        lower_cycle = jnp.maximum(cycle_index - 1, 0)
        upper_cycle = jnp.minimum(cycle_index + 1, CYCLES - 1)
        lower_block = lax.dynamic_slice_in_dim(loads, lower_cycle * DOF_CYCLE, DOF_CYCLE, 1)
        upper_block = lax.dynamic_slice_in_dim(loads, upper_cycle * DOF_CYCLE, DOF_CYCLE, 1)
        from_below = lower_block[:, iface[lower_cycle, 1], :].astype(jnp.float32) * (cycle_index > 0).astype(jnp.float32)
        from_above = upper_block[:, iface[upper_cycle, 0], :].astype(jnp.float32) * (cycle_index < CYCLES - 1).astype(jnp.float32)
        assembled = cycle_block.astype(jnp.float32).at[:, iface[cycle_index, 0], :].add(from_below)
        assembled = assembled.at[:, iface[cycle_index, 1], :].add(from_above).astype(jnp.bfloat16)
        spectrum = jnp.dot(forward, assembled.reshape(SECTORS, -1), preferred_element_type=jnp.float32)
        return spectrum.astype(jnp.bfloat16).reshape(SLOTS, 2, DOF_CYCLE, RHS)

    spectra = lax.map(assemble_cycle, jnp.arange(CYCLES, dtype=jnp.int32))

    def one_slot(slot_items):
        extended, weights, harmonic = slot_items
        return solve_slot(extended, weights[0], weights[1], harmonic == 0)

    def solve_cycle(cycle_index):
        lower_cycle = jnp.maximum(cycle_index - 1, 0)
        upper_cycle = jnp.minimum(cycle_index + 1, CYCLES - 1)
        own = spectra[cycle_index]
        above = jnp.where(cycle_index < CYCLES - 1, spectra[upper_cycle][:, :, iface[upper_cycle, 1], :], jnp.zeros((), jnp.bfloat16))
        below = jnp.where(cycle_index > 0, spectra[lower_cycle][:, :, iface[lower_cycle, 0], :], jnp.zeros((), jnp.bfloat16))
        extended = jnp.concatenate([own, above, below], axis=2)
        weights = lax.dynamic_slice_in_dim(factors, cycle_index * DOF_CYCLE, DOF_CYCLE, 2)
        return lax.map(one_slot, (extended, weights, assign))

    backs = lax.map(solve_cycle, jnp.arange(CYCLES, dtype=jnp.int32))

    def finish_cycle(cycle_index):
        offset = cycle_index * DOF_CYCLE
        lower_cycle = jnp.maximum(cycle_index - 1, 0)
        upper_cycle = jnp.minimum(cycle_index + 1, CYCLES - 1)
        own = backs[cycle_index][:, :, :DOF_CYCLE, :]
        got_lower = jnp.where(cycle_index > 0, backs[lower_cycle][:, :, DOF_CYCLE:DOF_CYCLE + FACE, :], jnp.zeros((), jnp.float32))
        got_upper = jnp.where(cycle_index < CYCLES - 1, backs[upper_cycle][:, :, DOF_CYCLE + FACE:, :], jnp.zeros((), jnp.float32))
        total = own.at[:, :, iface[cycle_index, 1], :].add(got_lower)
        total = total.at[:, :, iface[cycle_index, 0], :].add(got_upper).astype(jnp.bfloat16)
        adjoint = jnp.dot(inverse, total.reshape(SECTORS, -1), preferred_element_type=jnp.float32)
        adjoint = adjoint.astype(jnp.bfloat16).reshape(SECTORS, DOF_CYCLE, RHS)
        responses = lax.dynamic_slice_in_dim(state, offset, DOF_CYCLE, 1)
        return jnp.sum(adjoint.astype(jnp.float32) * responses.astype(jnp.float32), axis=-1)

    blocks = lax.map(finish_cycle, jnp.arange(CYCLES, dtype=jnp.int32))
    return jnp.transpose(blocks, (1, 0, 2)).reshape(SECTORS, DOFS)
```

```python
import math

import jax
import jax.numpy as jnp
from jax import lax
from jax.experimental import pallas as pl
from jax.experimental.pallas import tpu as pltpu
from jax.sharding import PartitionSpec as P

F32 = jnp.float32
BF16 = jnp.bfloat16
VMEM = pl.BlockSpec(memory_space=pltpu.VMEM)
SMEM = pl.BlockSpec(memory_space=pltpu.SMEM)
PARAMS = pltpu.CompilerParams(vmem_limit_bytes=48 * 1024 * 1024)
TILE = 16


def tables(assign, sectors):
    position = jnp.arange(sectors, dtype=jnp.int32)
    phases = assign[:, None] * position[None, :] % sectors
    angles = phases.astype(F32) * (2.0 * math.pi / sectors)
    paired = (assign == 0)[:, None]
    alternate = (1 - 2 * (position % 2)).astype(F32)[None, :]
    cos, sin = jnp.cos(angles), jnp.sin(angles)
    forward = jnp.stack([cos, jnp.where(paired, alternate, -sin)], axis=1)
    inverse = jnp.stack(
        [jnp.where(paired, 1.0, 2.0) * cos / sectors, jnp.where(paired, alternate, -2.0 * sin) / sectors],
        axis=1,
    )
    forward = forward.reshape(2 * assign.shape[0], sectors).astype(BF16)
    inverse = jnp.transpose(inverse.reshape(2 * assign.shape[0], sectors)).astype(BF16)
    return forward, inverse


def widen(table):
    eye = jnp.eye(TILE, dtype=BF16)
    side = table.shape[0] * TILE
    return (table[:, None, :, None] * eye[None, :, None, :]).reshape(side, side)


def dot(a, b):
    return jnp.dot(a, b, preferred_element_type=F32)


def transform_kernel(table_ref, x_ref, out_ref):
    count, rows, width = x_ref.shape
    for start in range(0, rows, TILE):
        tile = x_ref[:, start : start + TILE, :].reshape(count * TILE, width)
        out_ref[:, start : start + TILE, :] = (
            dot(table_ref[...], tile).astype(BF16).reshape(count, TILE, width)
        )


def transform(forward, pieces):
    rows = pieces.shape[1]
    if rows % TILE:
        return jnp.einsum("ks,sdr->kdr", forward, pieces, preferred_element_type=F32).astype(BF16)
    return pl.pallas_call(
        transform_kernel,
        out_shape=jax.ShapeDtypeStruct(pieces.shape, BF16),
        in_specs=[VMEM, VMEM],
        out_specs=VMEM,
        compiler_params=PARAMS,
        name="transform",
    )(widen(forward), pieces)


def respond_kernel(table_ref, x_ref, state_ref, out_ref):
    count, rows, width = x_ref.shape
    ones = jnp.ones((8, width), BF16)
    for index, start in enumerate(range(0, rows, TILE)):
        tile = x_ref[:, start : start + TILE, :].reshape(count * TILE, width)
        adjoint = dot(table_ref[...], tile).astype(BF16).astype(F32)
        state = state_ref[:, start : start + TILE, :].reshape(count * TILE, width).astype(F32)
        product = adjoint * state
        high = product.astype(BF16)
        low = (product - high.astype(F32)).astype(BF16)
        contract = (((1,), (1,)), ((), ()))
        total = lax.dot_general(ones, high, contract, preferred_element_type=F32)
        total = total + lax.dot_general(ones, low, contract, preferred_element_type=F32)
        out_ref[index : index + 1, :] = total[:1]


def respond(inverse, pieces, state):
    count, rows, _ = pieces.shape
    if rows % TILE:
        adjoint = jnp.einsum("sk,kdr->sdr", inverse, pieces, preferred_element_type=F32).astype(BF16)
        return jnp.sum(adjoint.astype(F32) * state.astype(F32), axis=-1)
    sums = pl.pallas_call(
        respond_kernel,
        out_shape=jax.ShapeDtypeStruct((rows // TILE, count * TILE), F32),
        in_specs=[VMEM, VMEM, VMEM],
        out_specs=VMEM,
        compiler_params=PARAMS,
        name="respond",
    )(widen(inverse), pieces, state)
    return sums.reshape(rows // TILE, count, TILE).transpose(1, 0, 2).reshape(count, rows)


def rows_of(x_ref, part):
    chunks, _, rows, width = x_ref.shape
    return x_ref[:, part].reshape(chunks * rows, width)


def faces_kernel(index_ref, x_ref, out_ref):
    count = index_ref.shape[0]
    cycle = x_ref.shape[0] * x_ref.shape[2]
    pick = index_ref[...] == lax.broadcasted_iota(jnp.int32, (count, cycle), 1)
    pick = jnp.where(pick, 1.0, 0.0).astype(BF16)
    for part in range(2):
        out_ref[part] = dot(pick, rows_of(x_ref, part)).astype(BF16)


def prepare_kernel(index_ref, weight_ref, out_ref):
    cycle = weight_ref.shape[1]
    count = index_ref.shape[1]
    pick = lax.broadcasted_iota(jnp.int32, (cycle, count), 0) == index_ref[...]
    pick = jnp.where(pick, 1.0, 0.0).astype(BF16)
    for part in range(2):
        out_ref[part] = dot(weight_ref[part, :, :cycle], pick).astype(BF16)


def right_sides(real, imag, paired):
    zero = jnp.zeros_like(imag)
    turned = jnp.where(paired, zero, imag)
    upper = jnp.concatenate([real, turned], axis=1)
    lower = jnp.concatenate([-turned, jnp.where(paired, imag, real)], axis=1)
    return upper, lower


def own_kernel(paired_ref, weight_ref, x_ref, out_ref):
    cycle = weight_ref.shape[1]
    upper, lower = right_sides(rows_of(x_ref, 0), rows_of(x_ref, 1), paired_ref[0] != 0)
    out_ref[...] = dot(weight_ref[0, :, :cycle], upper) + dot(weight_ref[1, :, :cycle], lower)


def back_sides(real, imag, paired):
    zero = jnp.zeros_like(imag)
    turned = jnp.where(paired, zero, imag)
    upper = jnp.concatenate([real, turned], axis=1)
    lower = jnp.concatenate([turned, jnp.where(paired, imag, -real)], axis=1)
    return upper, lower


def middle_kernel(paired_ref, own_ref, edge_ref, back_ref, near_ref, middle_ref, out_ref):
    paired = paired_ref[0] != 0
    width = near_ref.shape[2]
    upper, lower = right_sides(near_ref[0], near_ref[1], paired)
    middle = own_ref[...] + dot(edge_ref[0], upper) + dot(edge_ref[1], lower)
    middle = middle.astype(BF16)
    middle_ref[...] = middle
    upper, lower = back_sides(middle[:, :width], middle[:, width:], paired)
    out_ref[...] = (dot(back_ref[0], upper) + dot(back_ref[1], lower)).astype(BF16)


def back_kernel(paired_ref, turned_ref, middle_ref, out_ref):
    paired = paired_ref[0] != 0
    cycle = middle_ref.shape[0]
    width = middle_ref.shape[1] // 2
    upper, lower = back_sides(middle_ref[:, :width], middle_ref[:, width:], paired)
    out_ref[...] = dot(turned_ref[0, :cycle], upper) + dot(turned_ref[1, :cycle], lower)


def finish_kernel(index_ref, back_ref, got_ref, out_ref):
    chunks, _, rows, width = out_ref.shape
    cycle = back_ref.shape[0]
    count = index_ref.shape[1]
    pick = lax.broadcasted_iota(jnp.int32, (cycle, count), 0) == index_ref[...]
    pick = jnp.where(pick, 1.0, 0.0).astype(BF16)
    total = (back_ref[...] + dot(pick, got_ref[...])).astype(BF16)
    for part in range(2):
        out_ref[:, part] = total[:, part * width : (part + 1) * width].reshape(chunks, rows, width)


def call(kernel, outs, specs, name, *operands):
    return pl.pallas_call(
        kernel,
        out_shape=outs,
        in_specs=specs,
        out_specs=jax.tree.map(lambda _: VMEM, outs),
        compiler_params=PARAMS,
        name=name,
    )(*operands)


def per_device(loads, state, factors, assign, iface):
    local, cycle, width = loads.shape
    inner, outer = iface[0, 0], iface[0, 1]
    face = inner.shape[0]
    devices = lax.axis_size("sector")
    cycles = lax.axis_size("radial")
    here = lax.axis_index("radial")
    sectors = local * devices
    rows = cycle // devices
    aligned = rows % TILE == 0
    weight = factors[0]
    forward, inverse = tables(assign, sectors)
    paired = (assign[lax.axis_index("sector")] == 0).astype(jnp.int32).reshape(1)
    shape = jax.ShapeDtypeStruct

    def exchange(pieces):
        return lax.all_to_all(pieces, "sector", split_axis=0, concat_axis=0, tiled=True)

    def by_chunk(block):
        return block.reshape(local, devices, rows, width).transpose(1, 0, 2, 3)

    def step(block, shift):
        pairs = [(i, i + shift) for i in range(cycles) if 0 <= i + shift < cycles]
        return lax.ppermute(block, "radial", pairs)

    above = weight[:, :, cycle : cycle + face]
    below = weight[:, :, cycle + face :]
    if cycles == 2:
        low = here == 0
        toward = jnp.where(low, outer, inner)
        away = jnp.where(low, inner, outer)
        sent = jnp.concatenate([toward, away])
        gathered = toward
        scattered = away
        outward = jnp.where(low, above, below)
    else:
        sent = jnp.concatenate([inner, outer])
        gathered = jnp.concatenate([inner, outer])
        scattered = jnp.concatenate([outer, inner])
        outward = jnp.concatenate([above, below], axis=2)

    gains = call(
        prepare_kernel, shape((2, cycle, gathered.shape[0]), BF16), [VMEM, VMEM], "prepare",
        gathered.reshape(1, -1), weight,
    )
    edge = jnp.concatenate([gains, outward], axis=2)
    turned = jnp.swapaxes(weight, 1, 2)
    outward_turned = jnp.swapaxes(outward, 1, 2)

    pieces = exchange(by_chunk(loads)).reshape(sectors, rows, width)
    spectrum = transform(forward, pieces)
    harmonic = exchange(spectrum.reshape(devices, 2, rows, width))

    harmonic, state = lax.optimization_barrier((harmonic, state))
    state = exchange(by_chunk(state)).reshape(sectors, rows, width)

    if not aligned:
        harmonic = harmonic.transpose(1, 0, 2, 3).reshape(1, 2, cycle, width)
    faces = call(
        faces_kernel, shape((2, 2 * face, width), BF16), [VMEM, VMEM], "faces",
        sent.reshape(-1, 1), harmonic,
    )
    own = call(
        own_kernel, shape((cycle, 2 * width), F32), [SMEM, VMEM, VMEM], "own", paired, weight, harmonic
    )
    if cycles == 2:
        near = lax.ppermute(faces, "radial", [(0, 1), (1, 0)])
    else:
        lower = step(faces, 1)
        upper = step(faces, -1)
        beyond_above = step(faces[:, :face], -2)
        beyond_below = step(faces[:, face:], 2)
        far_above = (upper[:, face:].astype(F32) + beyond_above.astype(F32)).astype(BF16)
        far_below = (lower[:, :face].astype(F32) + beyond_below.astype(F32)).astype(BF16)
        near = jnp.concatenate([lower[:, face:], upper[:, :face], far_above, far_below], axis=1)
    middle, leaving = call(
        middle_kernel,
        (shape((cycle, 2 * width), BF16), shape((outward.shape[2], 2 * width), BF16)),
        [SMEM, VMEM, VMEM, VMEM, VMEM], "middle",
        paired, own, edge, outward_turned, near,
    )
    if cycles == 2:
        got = lax.ppermute(leaving, "radial", [(0, 1), (1, 0)])
    else:
        got = jnp.concatenate([step(leaving[:face], 1), step(leaving[face:], -1)], axis=0)
    back = call(
        back_kernel, shape((cycle, 2 * width), F32), [SMEM, VMEM, VMEM], "back", paired, turned, middle
    )
    solved = call(
        finish_kernel, shape((devices, 2, rows, width) if aligned else (1, 2, cycle, width), BF16),
        [VMEM, VMEM, VMEM], "finish", scattered.reshape(1, -1), back, got,
    )
    if not aligned:
        solved = solved.reshape(2, devices, rows, width).transpose(1, 0, 2, 3)
    pieces = exchange(solved).reshape(sectors, rows, width)
    found = respond(inverse, pieces, state).reshape(devices, local, rows)
    return exchange(found).transpose(1, 0, 2).reshape(local, cycle)


def solution(mesh):
    return jax.shard_map(
        per_device,
        mesh=mesh,
        in_specs=(
            P("sector", "radial", None),
            P("sector", "radial", None),
            P("sector", None, "radial", None),
            P(),
            P("radial", None, None),
        ),
        out_specs=P("sector", "radial"),
        check_vma=False,
    )
```

```python
import math

import jax
import jax.numpy as jnp
from jax import lax
from jax.experimental import pallas as pl
from jax.experimental.pallas import tpu as pltpu
from jax.sharding import PartitionSpec as P

F32 = jnp.float32
BF16 = jnp.bfloat16
VMEM = pl.BlockSpec(memory_space=pltpu.VMEM)
SMEM = pl.BlockSpec(memory_space=pltpu.SMEM)
ANY = pl.BlockSpec(memory_space=pl.ANY)
TILE = 16


def tables(assign, sectors):
    position = jnp.arange(sectors, dtype=jnp.int32)
    phases = assign[:, None] * position[None, :] % sectors
    angles = phases.astype(F32) * (2.0 * math.pi / sectors)
    paired = (assign == 0)[:, None]
    alternate = (1 - 2 * (position % 2)).astype(F32)[None, :]
    cos, sin = jnp.cos(angles), jnp.sin(angles)
    forward = jnp.stack([cos, jnp.where(paired, alternate, -sin)], axis=1)
    inverse = jnp.stack(
        [jnp.where(paired, 1.0, 2.0) * cos / sectors, jnp.where(paired, alternate, -2.0 * sin) / sectors],
        axis=1,
    )
    forward = forward.reshape(2 * assign.shape[0], sectors).astype(BF16)
    inverse = jnp.transpose(inverse.reshape(2 * assign.shape[0], sectors)).astype(BF16)
    return forward, inverse


def dot(a, b):
    return jnp.dot(a, b, preferred_element_type=F32)


def transform_kernel(table_ref, x_ref, out_ref):
    count, rows, width = x_ref.shape
    for start in range(0, rows, TILE):
        tile = x_ref[:, start : start + TILE, :].reshape(count * TILE, width)
        out_ref[:, start : start + TILE, :] = (
            dot(table_ref[...], tile).astype(BF16).reshape(count, TILE, width)
        )


def transform(table, pieces):
    rows = pieces.shape[1]
    if rows % TILE:
        return jnp.einsum("ks,sdr->kdr", table, pieces, preferred_element_type=F32).astype(BF16)
    return call(
        transform_kernel, jax.ShapeDtypeStruct(pieces.shape, BF16), [VMEM, VMEM], "transform", 8, table, pieces
    )


def respond_kernel(table_ref, x_ref, state_ref, out_ref):
    count, rows, width = x_ref.shape
    lanes = 128
    ones = jnp.ones((width, lanes), BF16)
    place = lax.broadcasted_iota(jnp.int32, (count * TILE, lanes), 0) % lanes
    diagonal = place == lax.broadcasted_iota(jnp.int32, (count * TILE, lanes), 1)
    for index, start in enumerate(range(0, rows, TILE)):
        tile = x_ref[:, start : start + TILE, :].reshape(count * TILE, width)
        adjoint = dot(table_ref[...], tile).astype(BF16).astype(F32)
        state = state_ref[:, start : start + TILE, :].reshape(count * TILE, width).astype(F32)
        product = adjoint * state
        high = product.astype(BF16)
        low = (product - high.astype(F32)).astype(BF16)
        total = jnp.where(diagonal, dot(high, ones) + dot(low, ones), 0.0)
        out_ref[index] = jnp.sum(total.reshape(count * TILE // lanes, lanes, lanes), axis=1)


def respond(table, pieces, state):
    count, rows, _ = pieces.shape
    if rows % TILE:
        adjoint = jnp.einsum("sk,kdr->sdr", table, pieces, preferred_element_type=F32).astype(BF16)
        return jnp.sum(adjoint.astype(F32) * state.astype(F32), axis=-1)
    sums = call(
        respond_kernel, jax.ShapeDtypeStruct((rows // TILE, count * TILE // 128, 128), F32),
        [VMEM, VMEM, VMEM], "respond", 12, table, pieces, state,
    )
    return sums.reshape(rows // TILE, count, TILE).transpose(1, 0, 2).reshape(count, rows)


def rows_of(x_ref, part):
    chunks, _, rows, width = x_ref.shape
    return x_ref[:, part].reshape(chunks * rows, width)


def faces_kernel(index_ref, x_ref, out_ref):
    count = index_ref.shape[0]
    cycle = x_ref.shape[0] * x_ref.shape[2]
    pick = index_ref[...] == lax.broadcasted_iota(jnp.int32, (count, cycle), 1)
    pick = jnp.where(pick, 1.0, 0.0).astype(BF16)
    for part in range(2):
        out_ref[part] = dot(pick, rows_of(x_ref, part)).astype(BF16)


def widen(table):
    count = table.shape[0]
    side = count * TILE
    spread = lax.broadcasted_iota(jnp.int32, (side, count), 0) // TILE
    spread = spread == lax.broadcasted_iota(jnp.int32, (side, count), 1)
    spread = jnp.where(spread, 1.0, 0.0).astype(BF16)
    tall = dot(spread, table).astype(BF16)
    full = lax.dot_general(tall, spread, (((1,), (1,)), ((), ())), preferred_element_type=F32)
    row = lax.broadcasted_iota(jnp.int32, (side, side), 0) % TILE
    column = lax.broadcasted_iota(jnp.int32, (side, side), 1) % TILE
    return jnp.where(row == column, full, 0.0).astype(BF16)


def widen_kernel(forward_ref, inverse_ref, forward_out, inverse_out):
    forward_out[...] = widen(forward_ref[...])
    inverse_out[...] = widen(inverse_ref[...])


def prepare_kernel(low_ref, index_ref, weight_ref, edge_ref, turned_ref, away_ref):
    cycle = weight_ref.shape[1]
    count = index_ref.shape[1]
    leaving = away_ref.shape[1]
    face = (weight_ref.shape[2] - cycle) // 2
    pick = lax.broadcasted_iota(jnp.int32, (cycle, count), 0) == index_ref[...]
    pick = jnp.where(pick, 1.0, 0.0).astype(BF16)
    for part in range(2):
        own = weight_ref[part, :, :cycle]
        outward = weight_ref[part, :, cycle:]
        if leaving == face:
            outward = jnp.where(low_ref[0] != 0, outward[:, :face], outward[:, face:])
        edge_ref[part, :, :count] = dot(own, pick).astype(BF16)
        edge_ref[part, :, count:] = outward
        turned_ref[part] = own.T
        away_ref[part] = outward.T


def chunk_kernel(x_ref, out_ref, sems):
    local = x_ref.shape[0]
    copies = [pltpu.make_async_copy(x_ref.at[i], out_ref.at[:, i], sems.at[i]) for i in range(local)]
    for copy in copies:
        copy.start()
    for copy in copies:
        copy.wait()


def by_chunk(block, devices):
    local, cycle, width = block.shape
    rows = cycle // devices
    split = block.reshape(local, devices, rows, width)
    if rows % TILE:
        return split.transpose(1, 0, 2, 3)
    return pl.pallas_call(
        chunk_kernel,
        out_shape=jax.ShapeDtypeStruct((devices, local, rows, width), block.dtype),
        in_specs=[ANY],
        out_specs=ANY,
        scratch_shapes=[pltpu.SemaphoreType.DMA((local,))],
        name="chunk",
    )(split)


def right_sides(real, imag, paired):
    zero = jnp.zeros_like(imag)
    turned = jnp.where(paired, zero, imag)
    upper = jnp.concatenate([real, turned], axis=1)
    lower = jnp.concatenate([-turned, jnp.where(paired, imag, real)], axis=1)
    return upper, lower


def own_kernel(paired_ref, weight_ref, x_ref, out_ref):
    cycle = weight_ref.shape[1]
    upper, lower = right_sides(rows_of(x_ref, 0), rows_of(x_ref, 1), paired_ref[0] != 0)
    out_ref[...] = dot(weight_ref[0, :, :cycle], upper) + dot(weight_ref[1, :, :cycle], lower)


def back_sides(real, imag, paired):
    zero = jnp.zeros_like(imag)
    turned = jnp.where(paired, zero, imag)
    upper = jnp.concatenate([real, turned], axis=1)
    lower = jnp.concatenate([turned, jnp.where(paired, imag, -real)], axis=1)
    return upper, lower


def middle_kernel(paired_ref, own_ref, edge_ref, back_ref, near_ref, middle_ref, out_ref):
    paired = paired_ref[0] != 0
    width = near_ref.shape[2]
    upper, lower = right_sides(near_ref[0], near_ref[1], paired)
    middle = own_ref[...] + dot(edge_ref[0], upper) + dot(edge_ref[1], lower)
    middle = middle.astype(BF16)
    middle_ref[...] = middle
    upper, lower = back_sides(middle[:, :width], middle[:, width:], paired)
    out_ref[...] = (dot(back_ref[0], upper) + dot(back_ref[1], lower)).astype(BF16)


def back_kernel(paired_ref, turned_ref, middle_ref, out_ref):
    paired = paired_ref[0] != 0
    width = middle_ref.shape[1] // 2
    upper, lower = back_sides(middle_ref[:, :width], middle_ref[:, width:], paired)
    out_ref[...] = dot(turned_ref[0], upper) + dot(turned_ref[1], lower)


def finish_kernel(index_ref, back_ref, got_ref, out_ref):
    chunks, _, rows, width = out_ref.shape
    cycle = back_ref.shape[0]
    count = index_ref.shape[1]
    pick = lax.broadcasted_iota(jnp.int32, (cycle, count), 0) == index_ref[...]
    pick = jnp.where(pick, 1.0, 0.0).astype(BF16)
    total = (back_ref[...] + dot(pick, got_ref[...])).astype(BF16)
    for part in range(2):
        out_ref[:, part] = total[:, part * width : (part + 1) * width].reshape(chunks, rows, width)


def call(kernel, outs, specs, name, mebibytes, *operands):
    return pl.pallas_call(
        kernel,
        out_shape=outs,
        in_specs=specs,
        out_specs=jax.tree.map(lambda _: VMEM, outs),
        compiler_params=pltpu.CompilerParams(vmem_limit_bytes=mebibytes * 1024 * 1024),
        name=name,
    )(*operands)


def per_device(loads, state, factors, assign, iface):
    local, cycle, width = loads.shape
    inner, outer = iface[0, 0], iface[0, 1]
    face = inner.shape[0]
    devices = lax.axis_size("sector")
    cycles = lax.axis_size("radial")
    here = lax.axis_index("radial")
    sectors = local * devices
    rows = cycle // devices
    aligned = rows % TILE == 0
    weight = factors[0]
    forward, inverse = tables(assign, sectors)
    paired = (assign[lax.axis_index("sector")] == 0).astype(jnp.int32).reshape(1)
    shape = jax.ShapeDtypeStruct

    def exchange(pieces):
        return lax.all_to_all(pieces, "sector", split_axis=0, concat_axis=0, tiled=True)

    def step(block, shift):
        pairs = [(i, i + shift) for i in range(cycles) if 0 <= i + shift < cycles]
        return lax.ppermute(block, "radial", pairs)

    if cycles == 2:
        toward = jnp.where(here == 0, outer, inner)
        away = jnp.where(here == 0, inner, outer)
        sent = jnp.concatenate([toward, away])
        gathered, scattered = toward, away
    else:
        sent = gathered = jnp.concatenate([inner, outer])
        scattered = jnp.concatenate([outer, inner])
    sent = sent.reshape(-1, 1)
    scattered = scattered.reshape(1, -1)
    edges = gathered.shape[0]

    pieces = exchange(by_chunk(loads, devices)).reshape(sectors, rows, width)

    edge, turned, outward = call(
        prepare_kernel,
        (shape((2, cycle, 2 * edges), BF16), shape((2, cycle, cycle), BF16), shape((2, edges, cycle), BF16)),
        [SMEM, VMEM, VMEM], "prepare", 20,
        (here == 0).astype(jnp.int32).reshape(1), gathered.reshape(1, -1), weight,
    )
    if aligned:
        wide = shape((sectors * TILE, sectors * TILE), BF16)
        forward, inverse = call(widen_kernel, (wide, wide), [VMEM, VMEM], "widen", 12, forward, inverse)
    state = by_chunk(state, devices)
    ready = (pieces, edge, turned, outward, forward, inverse, state, sent, scattered, paired)
    pieces, edge, turned, outward, forward, inverse, state, sent, scattered, paired = (
        lax.optimization_barrier(ready)
    )

    spectrum = transform(forward, pieces)
    harmonic = exchange(spectrum.reshape(devices, 2, rows, width))

    harmonic, state = lax.optimization_barrier((harmonic, state))
    state = exchange(state).reshape(sectors, rows, width)

    if not aligned:
        harmonic = harmonic.transpose(1, 0, 2, 3).reshape(1, 2, cycle, width)
    faces = call(
        faces_kernel, shape((2, 2 * face, width), BF16), [VMEM, VMEM], "faces", 8, sent, harmonic,
    )
    own = call(
        own_kernel, shape((cycle, 2 * width), F32), [SMEM, VMEM, VMEM], "own", 12, paired, weight, harmonic
    )
    if cycles == 2:
        near = lax.ppermute(faces, "radial", [(0, 1), (1, 0)])
    else:
        lower = step(faces, 1)
        upper = step(faces, -1)
        beyond_above = step(faces[:, :face], -2)
        beyond_below = step(faces[:, face:], 2)
        far_above = (upper[:, face:].astype(F32) + beyond_above.astype(F32)).astype(BF16)
        far_below = (lower[:, :face].astype(F32) + beyond_below.astype(F32)).astype(BF16)
        near = jnp.concatenate([lower[:, face:], upper[:, :face], far_above, far_below], axis=1)
    middle, leaving = call(
        middle_kernel,
        (shape((cycle, 2 * width), BF16), shape((edges, 2 * width), BF16)),
        [SMEM, VMEM, VMEM, VMEM, VMEM], "middle", 12,
        paired, own, edge, outward, near,
    )
    if cycles == 2:
        got = lax.ppermute(leaving, "radial", [(0, 1), (1, 0)])
    else:
        got = jnp.concatenate([step(leaving[:face], 1), step(leaving[face:], -1)], axis=0)
    back = call(
        back_kernel, shape((cycle, 2 * width), F32), [SMEM, VMEM, VMEM], "back", 12, paired, turned, middle
    )
    solved = call(
        finish_kernel, shape((devices, 2, rows, width) if aligned else (1, 2, cycle, width), BF16),
        [VMEM, VMEM, VMEM], "finish", 12, scattered, back, got,
    )
    if not aligned:
        solved = solved.reshape(2, devices, rows, width).transpose(1, 0, 2, 3)
    pieces = exchange(solved).reshape(sectors, rows, width)
    found = respond(inverse, pieces, state).reshape(devices, local, rows)
    return exchange(found).transpose(1, 0, 2).reshape(local, cycle)


def solution(mesh):
    return jax.shard_map(
        per_device,
        mesh=mesh,
        in_specs=(
            P("sector", "radial", None),
            P("sector", "radial", None),
            P("sector", None, "radial", None),
            P(),
            P("radial", None, None),
        ),
        out_specs=P("sector", "radial"),
        check_vma=False,
    )
```

```python
import math

import jax
import jax.numpy as jnp
from jax import lax
from jax.experimental import pallas as pl
from jax.experimental.pallas import tpu as pltpu
from jax.sharding import PartitionSpec as P

F32 = jnp.float32
BF16 = jnp.bfloat16
VMEM = pl.BlockSpec(memory_space=pltpu.VMEM)
SMEM = pl.BlockSpec(memory_space=pltpu.SMEM)
ANY = pl.BlockSpec(memory_space=pl.ANY)
TILE = 16
TOKEN = jax.ShapeDtypeStruct((8, 128), jnp.float32)


def tables(assign, sectors):
    position = jnp.arange(sectors, dtype=jnp.int32)
    phases = assign[:, None] * position[None, :] % sectors
    angles = phases.astype(F32) * (2.0 * math.pi / sectors)
    paired = (assign == 0)[:, None]
    alternate = (1 - 2 * (position % 2)).astype(F32)[None, :]
    cos, sin = jnp.cos(angles), jnp.sin(angles)
    forward = jnp.stack([cos, jnp.where(paired, alternate, -sin)], axis=1)
    inverse = jnp.stack(
        [jnp.where(paired, 1.0, 2.0) * cos / sectors, jnp.where(paired, alternate, -2.0 * sin) / sectors],
        axis=1,
    )
    forward = forward.reshape(2 * assign.shape[0], sectors).astype(BF16)
    inverse = jnp.transpose(inverse.reshape(2 * assign.shape[0], sectors)).astype(BF16)
    return forward, inverse


def dot(a, b):
    return jnp.dot(a, b, preferred_element_type=F32)


def transform_kernel(table_ref, x_ref, out_ref, token_ref):
    count, rows, width = x_ref.shape
    token_ref[...] = jnp.zeros_like(token_ref)
    for start in range(0, rows, TILE):
        tile = x_ref[:, start : start + TILE, :].reshape(count * TILE, width)
        out_ref[:, start : start + TILE, :] = (
            dot(table_ref[...], tile).astype(BF16).reshape(count, TILE, width)
        )


def transform(table, pieces):
    rows = pieces.shape[1]
    if rows % TILE:
        out = jnp.einsum("ks,sdr->kdr", table, pieces, preferred_element_type=F32).astype(BF16)
        return out, jnp.zeros(TOKEN.shape, TOKEN.dtype)
    return call(
        transform_kernel, (jax.ShapeDtypeStruct(pieces.shape, BF16), TOKEN), [VMEM, VMEM], "transform", 8,
        table, pieces,
    )


def respond_kernel(table_ref, x_ref, far_ref, out_ref, state_ref, sems):
    count, rows, width = x_ref.shape
    copies = []
    for index, start in enumerate(range(0, rows, TILE)):
        span = slice(start, start + TILE)
        copies.append(pltpu.make_async_copy(far_ref.at[:, span], state_ref.at[:, span], sems.at[index]))
        copies[-1].start()
    lanes = 128
    ones = jnp.ones((width, lanes), BF16)
    place = lax.broadcasted_iota(jnp.int32, (count * TILE, lanes), 0) % lanes
    diagonal = place == lax.broadcasted_iota(jnp.int32, (count * TILE, lanes), 1)
    for index, start in enumerate(range(0, rows, TILE)):
        tile = x_ref[:, start : start + TILE, :].reshape(count * TILE, width)
        adjoint = dot(table_ref[...], tile).astype(BF16).astype(F32)
        copies[index].wait()
        state = state_ref[:, start : start + TILE, :].reshape(count * TILE, width).astype(F32)
        product = adjoint * state
        high = product.astype(BF16)
        low = (product - high.astype(F32)).astype(BF16)
        total = jnp.where(diagonal, dot(high, ones) + dot(low, ones), 0.0)
        out_ref[index] = jnp.sum(total.reshape(count * TILE // lanes, lanes, lanes), axis=1)


def respond(table, pieces, state):
    count, rows, _ = pieces.shape
    if rows % TILE:
        adjoint = jnp.einsum("sk,kdr->sdr", table, pieces, preferred_element_type=F32).astype(BF16)
        return jnp.sum(adjoint.astype(F32) * state.astype(F32), axis=-1)
    sums = call(
        respond_kernel, jax.ShapeDtypeStruct((rows // TILE, count * TILE // 128, 128), F32),
        [VMEM, VMEM, ANY], "respond", 12, table, pieces, state,
        scratch=(pltpu.VMEM(state.shape, BF16), pltpu.SemaphoreType.DMA((rows // TILE,))),
    )
    return sums.reshape(rows // TILE, count, TILE).transpose(1, 0, 2).reshape(count, rows)


def rows_of(x_ref, part):
    chunks, _, rows, width = x_ref.shape
    return x_ref[:, part].reshape(chunks * rows, width)


def faces_kernel(index_ref, x_ref, out_ref, token_ref):
    token_ref[...] = jnp.zeros_like(token_ref)
    count = index_ref.shape[0]
    cycle = x_ref.shape[0] * x_ref.shape[2]
    pick = index_ref[...] == lax.broadcasted_iota(jnp.int32, (count, cycle), 1)
    pick = jnp.where(pick, 1.0, 0.0).astype(BF16)
    for part in range(2):
        out_ref[part] = dot(pick, rows_of(x_ref, part)).astype(BF16)


def widen(table):
    count = table.shape[0]
    side = count * TILE
    spread = lax.broadcasted_iota(jnp.int32, (side, count), 0) // TILE
    spread = spread == lax.broadcasted_iota(jnp.int32, (side, count), 1)
    spread = jnp.where(spread, 1.0, 0.0).astype(BF16)
    tall = dot(spread, table).astype(BF16)
    full = lax.dot_general(tall, spread, (((1,), (1,)), ((), ())), preferred_element_type=F32)
    row = lax.broadcasted_iota(jnp.int32, (side, side), 0) % TILE
    column = lax.broadcasted_iota(jnp.int32, (side, side), 1) % TILE
    return jnp.where(row == column, full, 0.0).astype(BF16)


def widen_kernel(forward_ref, inverse_ref, forward_out, inverse_out):
    forward_out[...] = widen(forward_ref[...])
    inverse_out[...] = widen(inverse_ref[...])


def prepare_kernel(low_ref, index_ref, weight_ref, edge_ref, turned_ref, away_ref):
    cycle = weight_ref.shape[1]
    count = index_ref.shape[1]
    leaving = away_ref.shape[1]
    face = (weight_ref.shape[2] - cycle) // 2
    pick = lax.broadcasted_iota(jnp.int32, (cycle, count), 0) == index_ref[...]
    pick = jnp.where(pick, 1.0, 0.0).astype(BF16)
    for part in range(2):
        own = weight_ref[part, :, :cycle]
        outward = weight_ref[part, :, cycle:]
        if leaving == face:
            outward = jnp.where(low_ref[0] != 0, outward[:, :face], outward[:, face:])
        edge_ref[part, :, :count] = dot(own, pick).astype(BF16)
        edge_ref[part, :, count:] = outward
        turned_ref[part] = own.T
        away_ref[part] = outward.T


def chunk_kernel(token_ref, x_ref, out_ref, sems):
    local, devices = x_ref.shape[:2]
    step = devices // sems.shape[1]
    copies = []
    for i in range(local):
        for j in range(sems.shape[1]):
            span = slice(j * step, (j + 1) * step)
            copies.append(pltpu.make_async_copy(x_ref.at[i, span], out_ref.at[span, i], sems.at[i, j]))
            copies[-1].start()
    for copy in copies:
        copy.wait()


def by_chunk(block, devices, token):
    local, cycle, width = block.shape
    rows = cycle // devices
    split = block.reshape(local, devices, rows, width)
    if rows % TILE or devices % 4:
        return split.transpose(1, 0, 2, 3)
    return call(
        chunk_kernel, jax.ShapeDtypeStruct((devices, local, rows, width), block.dtype), [ANY, ANY], "chunk", 8,
        token, split, scratch=(pltpu.SemaphoreType.DMA((local, 4)),),
    )


def right_sides(real, imag, paired):
    zero = jnp.zeros_like(imag)
    turned = jnp.where(paired, zero, imag)
    upper = jnp.concatenate([real, turned], axis=1)
    lower = jnp.concatenate([-turned, jnp.where(paired, imag, real)], axis=1)
    return upper, lower


def own_kernel(paired_ref, weight_ref, x_ref, out_ref):
    cycle = weight_ref.shape[1]
    upper, lower = right_sides(rows_of(x_ref, 0), rows_of(x_ref, 1), paired_ref[0] != 0)
    out_ref[...] = dot(weight_ref[0, :, :cycle], upper) + dot(weight_ref[1, :, :cycle], lower)


def back_sides(real, imag, paired):
    zero = jnp.zeros_like(imag)
    turned = jnp.where(paired, zero, imag)
    upper = jnp.concatenate([real, turned], axis=1)
    lower = jnp.concatenate([turned, jnp.where(paired, imag, -real)], axis=1)
    return upper, lower


def middle_kernel(paired_ref, own_ref, edge_ref, back_ref, near_ref, middle_ref, out_ref):
    paired = paired_ref[0] != 0
    width = near_ref.shape[2]
    upper, lower = right_sides(near_ref[0], near_ref[1], paired)
    middle = own_ref[...] + dot(edge_ref[0], upper) + dot(edge_ref[1], lower)
    middle = middle.astype(BF16)
    middle_ref[...] = middle
    upper, lower = back_sides(middle[:, :width], middle[:, width:], paired)
    out_ref[...] = (dot(back_ref[0], upper) + dot(back_ref[1], lower)).astype(BF16)


def back_kernel(paired_ref, turned_ref, middle_ref, out_ref):
    paired = paired_ref[0] != 0
    width = middle_ref.shape[1] // 2
    upper, lower = back_sides(middle_ref[:, :width], middle_ref[:, width:], paired)
    out_ref[...] = dot(turned_ref[0], upper) + dot(turned_ref[1], lower)


def finish_kernel(index_ref, back_ref, got_ref, out_ref):
    chunks, _, rows, width = out_ref.shape
    cycle = back_ref.shape[0]
    count = index_ref.shape[1]
    pick = lax.broadcasted_iota(jnp.int32, (cycle, count), 0) == index_ref[...]
    pick = jnp.where(pick, 1.0, 0.0).astype(BF16)
    total = (back_ref[...] + dot(pick, got_ref[...])).astype(BF16)
    for part in range(2):
        out_ref[:, part] = total[:, part * width : (part + 1) * width].reshape(chunks, rows, width)


def call(kernel, outs, specs, name, mebibytes, *operands, scratch=()):
    return pl.pallas_call(
        kernel,
        out_shape=outs,
        in_specs=specs,
        out_specs=jax.tree.map(lambda _: VMEM, outs),
        scratch_shapes=scratch,
        compiler_params=pltpu.CompilerParams(vmem_limit_bytes=mebibytes * 1024 * 1024),
        name=name,
    )(*operands)


def per_device(loads, state, factors, assign, iface):
    local, cycle, width = loads.shape
    inner, outer = iface[0, 0], iface[0, 1]
    face = inner.shape[0]
    devices = lax.axis_size("sector")
    cycles = lax.axis_size("radial")
    here = lax.axis_index("radial")
    sectors = local * devices
    rows = cycle // devices
    aligned = rows % TILE == 0
    weight = factors[0]
    forward, inverse = tables(assign, sectors)
    paired = (assign[lax.axis_index("sector")] == 0).astype(jnp.int32).reshape(1)
    shape = jax.ShapeDtypeStruct

    def exchange(pieces):
        return lax.all_to_all(pieces, "sector", split_axis=0, concat_axis=0, tiled=True)

    def step(block, shift):
        pairs = [(i, i + shift) for i in range(cycles) if 0 <= i + shift < cycles]
        return lax.ppermute(block, "radial", pairs)

    if cycles == 2:
        toward = jnp.where(here == 0, outer, inner)
        away = jnp.where(here == 0, inner, outer)
        sent = jnp.concatenate([toward, away])
        gathered, scattered = toward, away
    else:
        sent = gathered = jnp.concatenate([inner, outer])
        scattered = jnp.concatenate([outer, inner])
    sent = sent.reshape(-1, 1)
    scattered = scattered.reshape(1, -1)
    edges = gathered.shape[0]

    pieces = exchange(by_chunk(loads, devices, jnp.zeros(TOKEN.shape, TOKEN.dtype))).reshape(sectors, rows, width)

    edge, turned, outward = call(
        prepare_kernel,
        (shape((2, cycle, 2 * edges), BF16), shape((2, cycle, cycle), BF16), shape((2, edges, cycle), BF16)),
        [SMEM, VMEM, VMEM], "prepare", 20,
        (here == 0).astype(jnp.int32).reshape(1), gathered.reshape(1, -1), weight,
    )
    if aligned:
        wide = shape((sectors * TILE, sectors * TILE), BF16)
        forward, inverse = call(widen_kernel, (wide, wide), [VMEM, VMEM], "widen", 12, forward, inverse)
    spectrum, token = transform(forward, pieces)
    harmonic = exchange(spectrum.reshape(devices, 2, rows, width))
    state = by_chunk(state, devices, token)

    if not aligned:
        harmonic = harmonic.transpose(1, 0, 2, 3).reshape(1, 2, cycle, width)
    faces, token = call(
        faces_kernel, (shape((2, 2 * face, width), BF16), TOKEN), [VMEM, VMEM], "faces", 8, sent, harmonic
    )
    state, _ = lax.optimization_barrier((state, token))
    state = exchange(state).reshape(sectors, rows, width)
    own = call(
        own_kernel, shape((cycle, 2 * width), F32), [SMEM, VMEM, VMEM], "own", 12, paired, weight, harmonic
    )
    if cycles == 2:
        near = lax.ppermute(faces, "radial", [(0, 1), (1, 0)])
    else:
        lower = step(faces, 1)
        upper = step(faces, -1)
        beyond_above = step(faces[:, :face], -2)
        beyond_below = step(faces[:, face:], 2)
        far_above = (upper[:, face:].astype(F32) + beyond_above.astype(F32)).astype(BF16)
        far_below = (lower[:, :face].astype(F32) + beyond_below.astype(F32)).astype(BF16)
        near = jnp.concatenate([lower[:, face:], upper[:, :face], far_above, far_below], axis=1)
    middle, leaving = call(
        middle_kernel,
        (shape((cycle, 2 * width), BF16), shape((edges, 2 * width), BF16)),
        [SMEM, VMEM, VMEM, VMEM, VMEM], "middle", 12,
        paired, own, edge, outward, near,
    )
    if cycles == 2:
        got = lax.ppermute(leaving, "radial", [(0, 1), (1, 0)])
    else:
        got = jnp.concatenate([step(leaving[:face], 1), step(leaving[face:], -1)], axis=0)
    back = call(
        back_kernel, shape((cycle, 2 * width), F32), [SMEM, VMEM, VMEM], "back", 12, paired, turned, middle
    )
    solved = call(
        finish_kernel, shape((devices, 2, rows, width) if aligned else (1, 2, cycle, width), BF16),
        [VMEM, VMEM, VMEM], "finish", 12, scattered, back, got,
    )
    if not aligned:
        solved = solved.reshape(2, devices, rows, width).transpose(1, 0, 2, 3)
    pieces = exchange(solved).reshape(sectors, rows, width)
    found = respond(inverse, pieces, state).reshape(devices, local, rows)
    return exchange(found).transpose(1, 0, 2).reshape(local, cycle)


def solution(mesh):
    return jax.shard_map(
        per_device,
        mesh=mesh,
        in_specs=(
            P("sector", "radial", None),
            P("sector", "radial", None),
            P("sector", None, "radial", None),
            P(),
            P("radial", None, None),
        ),
        out_specs=P("sector", "radial"),
        check_vma=False,
    )
```

```python
import math

import jax
import jax.numpy as jnp
from jax import lax
from jax.experimental import pallas as pl
from jax.experimental.pallas import tpu as pltpu
from jax.sharding import PartitionSpec as P

F32 = jnp.float32
BF16 = jnp.bfloat16
VMEM = pl.BlockSpec(memory_space=pltpu.VMEM)
SMEM = pl.BlockSpec(memory_space=pltpu.SMEM)
ANY = pl.BlockSpec(memory_space=pl.ANY)
HBM = pl.BlockSpec(memory_space=pltpu.HBM)
TILE = 16


def tables(assign, sectors):
    position = jnp.arange(sectors, dtype=jnp.int32)
    phases = assign[:, None] * position[None, :] % sectors
    angles = phases.astype(F32) * (2.0 * math.pi / sectors)
    paired = (assign == 0)[:, None]
    alternate = (1 - 2 * (position % 2)).astype(F32)[None, :]
    cos, sin = jnp.cos(angles), jnp.sin(angles)
    forward = jnp.stack([cos, jnp.where(paired, alternate, -sin)], axis=1)
    inverse = jnp.stack(
        [jnp.where(paired, 1.0, 2.0) * cos / sectors, jnp.where(paired, alternate, -2.0 * sin) / sectors],
        axis=1,
    )
    forward = forward.reshape(2 * assign.shape[0], sectors).astype(BF16)
    inverse = jnp.transpose(inverse.reshape(2 * assign.shape[0], sectors)).astype(BF16)
    return forward, inverse


def dot(a, b):
    return jnp.dot(a, b, preferred_element_type=F32)


def tiles(rows):
    return [slice(start, start + TILE) for start in range(0, rows, TILE)]


def transform_kernel(table_ref, x_ref, *refs):
    out_ref, held_ref, sems = refs[-3:]
    count, rows, width = x_ref.shape
    copies = []
    for index, span in enumerate(tiles(rows)):
        tile = x_ref[:, span, :].reshape(count * TILE, width)
        held_ref[index] = dot(table_ref[...], tile).astype(BF16).reshape(count, TILE, width)
        for part in range(2):
            half = slice(part * count // 2, (part + 1) * count // 2)
            copies.append(
                pltpu.make_async_copy(held_ref.at[index, half], out_ref.at[half, span], sems.at[index, part])
            )
            copies[-1].start()
    for copy in copies:
        copy.wait()


def transform(table, pieces, after):
    count, rows, width = pieces.shape
    if rows % TILE:
        return jnp.einsum("ks,sdr->kdr", table, pieces, preferred_element_type=F32).astype(BF16)
    steps = rows // TILE
    return call(
        transform_kernel, jax.ShapeDtypeStruct(pieces.shape, BF16), [VMEM, VMEM] + [ANY] * len(after), "transform", 8,
        table, pieces, *after, out_spaces=[pltpu.HBM],
        scratch=(pltpu.VMEM((steps, count, TILE, width), BF16), pltpu.SemaphoreType.DMA((steps, 2))),
    )


def stage_kernel(x_ref, out_ref, sems):
    step = x_ref.shape[0] // sems.shape[0]
    copies = []
    for j in range(sems.shape[0]):
        span = slice(j * step, (j + 1) * step)
        copies.append(pltpu.make_async_copy(x_ref.at[span], out_ref.at[span], sems.at[j]))
        copies[-1].start()
    for copy in copies:
        copy.wait()


def respond_kernel(table_ref, x_ref, state_ref, out_ref):
    count, rows, width = x_ref.shape
    lanes = 128
    place = lax.broadcasted_iota(jnp.int32, (count * TILE, lanes), 0) % lanes
    diagonal = place == lax.broadcasted_iota(jnp.int32, (count * TILE, lanes), 1)
    for index, span in enumerate(tiles(rows)):
        tile = x_ref[:, span, :].reshape(count * TILE, width)
        adjoint = dot(table_ref[...], tile).astype(BF16).astype(F32)
        state = state_ref[:, span, :].reshape(count * TILE, width).astype(F32)
        total = jnp.sum(adjoint * state, axis=1, keepdims=True)
        total = jnp.where(diagonal, total, 0.0)
        out_ref[index] = jnp.sum(total.reshape(count * TILE // lanes, lanes, lanes), axis=1)


def respond(table, pieces, state):
    count, rows, _ = pieces.shape
    if rows % TILE:
        adjoint = jnp.einsum("sk,kdr->sdr", table, pieces, preferred_element_type=F32).astype(BF16)
        return jnp.sum(adjoint.astype(F32) * state.astype(F32), axis=-1)
    sums = call(
        respond_kernel, jax.ShapeDtypeStruct((rows // TILE, count * TILE // 128, 128), F32),
        [VMEM, VMEM, VMEM], "respond", 12, table, pieces, state,
    )
    return sums.reshape(rows // TILE, count, TILE).transpose(1, 0, 2).reshape(count, rows)


def rows_of(x_ref, part):
    chunks, _, rows, width = x_ref.shape
    return x_ref[:, part].reshape(chunks * rows, width)


def fetch(x_ref, held_ref, sems):
    chunks, pieces = x_ref.shape[0], sems.shape[0]
    step = chunks // pieces
    copies = []
    for j in range(pieces):
        span = slice(j * step, (j + 1) * step)
        copies.append(pltpu.make_async_copy(x_ref.at[span], held_ref.at[span], sems.at[j]))
        copies[-1].start()
    return copies


def fetch_scratch(array):
    return pltpu.VMEM(array.shape, array.dtype), pltpu.SemaphoreType.DMA((math.gcd(array.shape[0], 8),))


def faces_kernel(index_ref, x_ref, out_ref, held_ref, sems):
    copies = fetch(x_ref, held_ref, sems)
    chunks, _, rows, width = x_ref.shape
    count = index_ref.shape[1]
    square = (count, count)
    diagonal = lax.broadcasted_iota(jnp.int32, square, 0) == lax.broadcasted_iota(jnp.int32, square, 1)
    column = jnp.sum(jnp.where(diagonal, index_ref[...].astype(F32), 0.0), axis=1, keepdims=True)
    pick = column.astype(jnp.int32) == lax.broadcasted_iota(jnp.int32, (count, chunks * rows), 1)
    pick = jnp.where(pick, 1.0, 0.0).astype(BF16)
    for copy in copies:
        copy.wait()
    for part in range(2):
        out_ref[part] = dot(pick, rows_of(held_ref, part)).astype(BF16)


def widen(table):
    count = table.shape[0]
    side = count * TILE
    spread = lax.broadcasted_iota(jnp.int32, (side, count), 0) // TILE
    spread = spread == lax.broadcasted_iota(jnp.int32, (side, count), 1)
    spread = jnp.where(spread, 1.0, 0.0).astype(BF16)
    tall = dot(spread, table).astype(BF16)
    full = lax.dot_general(tall, spread, (((1,), (1,)), ((), ())), preferred_element_type=F32)
    row = lax.broadcasted_iota(jnp.int32, (side, side), 0) % TILE
    column = lax.broadcasted_iota(jnp.int32, (side, side), 1) % TILE
    return jnp.where(row == column, full, 0.0).astype(BF16)


def widen_kernel(forward_ref, inverse_ref, forward_out, inverse_out):
    forward_out[...] = widen(forward_ref[...])
    inverse_out[...] = widen(inverse_ref[...])


def prepare_kernel(low_ref, index_ref, weight_ref, edge_ref, turned_ref, away_ref):
    cycle = weight_ref.shape[1]
    count = index_ref.shape[1]
    leaving = away_ref.shape[1]
    face = (weight_ref.shape[2] - cycle) // 2
    pick = lax.broadcasted_iota(jnp.int32, (cycle, count), 0) == index_ref[...]
    pick = jnp.where(pick, 1.0, 0.0).astype(BF16)
    for part in range(2):
        own = weight_ref[part, :, :cycle]
        outward = weight_ref[part, :, cycle:]
        if leaving == face:
            outward = jnp.where(low_ref[0] != 0, outward[:, :face], outward[:, face:])
        edge_ref[part, :, :count] = dot(own, pick).astype(BF16)
        edge_ref[part, :, count:] = outward
        turned_ref[part] = own.T
        away_ref[part] = outward.T


def chunk_kernel(x_ref, out_ref, sems):
    local, devices = x_ref.shape[:2]
    count = sems.shape[0]
    step = devices // count
    copies = []
    for j in range(count):
        span = slice(j * step, (j + 1) * step)
        for i in range(local):
            copies.append(pltpu.make_async_copy(x_ref.at[i, span], out_ref.at[span, i], sems.at[j, i]))
            copies[-1].start()
    for copy in copies:
        copy.wait()


def by_chunk(block, devices):
    local, cycle, width = block.shape
    rows = cycle // devices
    split = block.reshape(local, devices, rows, width)
    if rows % TILE or devices % 4:
        return split.transpose(1, 0, 2, 3)
    out = jax.ShapeDtypeStruct((devices, local, rows, width), block.dtype)
    return call(
        chunk_kernel, out, [HBM], "chunk", 8, split,
        scratch=(pltpu.SemaphoreType.DMA((4, local)),),
    )


GROUP = 4


def near_kernel(me_ref, x_ref, *refs):
    *outs, sems = refs
    copies = []
    for k in range(GROUP):
        member = me_ref[0] ^ k
        copies.append(pltpu.make_async_copy(x_ref.at[:, :, member], outs[k], sems.at[k]))
        copies[-1].start()
    for copy in copies:
        copy.wait()


def far_kernel(me_ref, *refs):
    blocks, out_ref, sems = refs[:GROUP], refs[GROUP], refs[GROUP + 1]
    local = blocks[0].shape[0]
    copies = []
    for j, block in enumerate(blocks):
        member = me_ref[0] ^ j
        for i in range(local):
            copies.append(pltpu.make_async_copy(block.at[i], out_ref.at[:, member * local + i], sems.at[j, i]))
            copies[-1].start()
    for copy in copies:
        copy.wait()


def right_sides(real, imag, paired):
    zero = jnp.zeros_like(imag)
    turned = jnp.where(paired, zero, imag)
    upper = jnp.concatenate([real, turned], axis=1)
    lower = jnp.concatenate([-turned, jnp.where(paired, imag, real)], axis=1)
    return upper, lower


def own_kernel(paired_ref, weight_ref, x_ref, out_ref, held_ref, sems):
    cycle = weight_ref.shape[1]
    for copy in fetch(x_ref, held_ref, sems):
        copy.wait()
    upper, lower = right_sides(rows_of(held_ref, 0), rows_of(held_ref, 1), paired_ref[0] != 0)
    out_ref[...] = dot(weight_ref[0, :, :cycle], upper) + dot(weight_ref[1, :, :cycle], lower)


def back_sides(real, imag, paired):
    zero = jnp.zeros_like(imag)
    turned = jnp.where(paired, zero, imag)
    upper = jnp.concatenate([real, turned], axis=1)
    lower = jnp.concatenate([turned, jnp.where(paired, imag, -real)], axis=1)
    return upper, lower


def middle_kernel(paired_ref, own_ref, edge_ref, back_ref, near_ref, middle_ref, out_ref):
    paired = paired_ref[0] != 0
    width = near_ref.shape[2]
    upper, lower = right_sides(near_ref[0], near_ref[1], paired)
    middle = own_ref[...] + dot(edge_ref[0], upper) + dot(edge_ref[1], lower)
    middle = middle.astype(BF16)
    middle_ref[...] = middle
    upper, lower = back_sides(middle[:, :width], middle[:, width:], paired)
    out_ref[...] = (dot(back_ref[0], upper) + dot(back_ref[1], lower)).astype(BF16)


def back_kernel(paired_ref, turned_ref, middle_ref, out_ref):
    paired = paired_ref[0] != 0
    width = middle_ref.shape[1] // 2
    upper, lower = back_sides(middle_ref[:, :width], middle_ref[:, width:], paired)
    out_ref[...] = dot(turned_ref[0], upper) + dot(turned_ref[1], lower)


def finish_kernel(index_ref, back_ref, got_ref, out_ref):
    chunks, _, rows, width = out_ref.shape
    cycle = back_ref.shape[0]
    count = index_ref.shape[1]
    pick = lax.broadcasted_iota(jnp.int32, (cycle, count), 0) == index_ref[...]
    pick = jnp.where(pick, 1.0, 0.0).astype(BF16)
    total = (back_ref[...] + dot(pick, got_ref[...])).astype(BF16)
    for part in range(2):
        out_ref[:, part] = total[:, part * width : (part + 1) * width].reshape(chunks, rows, width)


def placed(operand, spec):
    space = spec.memory_space
    return pltpu.with_memory_space_constraint(operand, space) if space in (pltpu.VMEM, pltpu.HBM) else operand


def call(kernel, outs, specs, name, mebibytes, *operands, scratch=(), out_spaces=None):
    single = not isinstance(outs, (list, tuple))
    shapes = [outs] if single else list(outs)
    spaces = out_spaces or [pltpu.VMEM] * len(shapes)
    results = pl.pallas_call(
        kernel,
        out_shape=[space(out.shape, out.dtype) for out, space in zip(shapes, spaces)],
        in_specs=specs,
        out_specs=[pl.BlockSpec(memory_space=space) for space in spaces],
        scratch_shapes=scratch,
        compiler_params=pltpu.CompilerParams(vmem_limit_bytes=mebibytes * 1024 * 1024),
        name=name,
    )(*(placed(operand, spec) for operand, spec in zip(operands, specs)))
    return results[0] if single else list(results)


def per_device(loads, state, factors, assign, iface):
    local, cycle, width = loads.shape
    inner, outer = iface[0, 0], iface[0, 1]
    face = inner.shape[0]
    devices = lax.axis_size("sector")
    cycles = lax.axis_size("radial")
    here = lax.axis_index("radial")
    sectors = local * devices
    rows = cycle // devices
    aligned = rows % TILE == 0
    weight = factors[0]
    forward, inverse = tables(assign, sectors)
    paired = (assign[lax.axis_index("sector")] == 0).astype(jnp.int32).reshape(1)
    shape = jax.ShapeDtypeStruct

    def exchange(pieces):
        return lax.all_to_all(pieces, "sector", split_axis=0, concat_axis=0, tiled=True)

    def step(block, shift):
        pairs = [(i, i + shift) for i in range(cycles) if 0 <= i + shift < cycles]
        return lax.ppermute(block, "radial", pairs)

    if cycles == 2:
        toward = jnp.where(here == 0, outer, inner)
        away = jnp.where(here == 0, inner, outer)
        sent = jnp.concatenate([toward, away])
        gathered, scattered = toward, away
    else:
        sent = gathered = jnp.concatenate([inner, outer])
        scattered = jnp.concatenate([outer, inner])
    sent = sent.reshape(1, -1)
    scattered = scattered.reshape(1, -1)
    edges = gathered.shape[0]

    pieces = exchange(by_chunk(loads, devices)).reshape(sectors, rows, width)

    edge, turned, outward = call(
        prepare_kernel,
        (shape((2, cycle, 2 * edges), BF16), shape((2, cycle, cycle), BF16), shape((2, edges, cycle), BF16)),
        [SMEM, VMEM, VMEM], "prepare", 20,
        (here == 0).astype(jnp.int32).reshape(1), gathered.reshape(1, -1), weight,
    )
    if aligned:
        wide = shape((sectors * TILE, sectors * TILE), BF16)
        forward, inverse = call(widen_kernel, (wide, wide), [VMEM, VMEM], "widen", 12, forward, inverse)
    groups = devices // GROUP
    by_groups = aligned and devices == groups * GROUP and groups > 1
    place = lax.axis_index("sector")
    member = (place % GROUP).astype(jnp.int32).reshape(1)
    group = (place // GROUP).astype(jnp.int32).reshape(1)
    blocks = []
    if by_groups:
        block = shape((local, groups, rows, width), BF16)
        blocks = call(
            near_kernel, [block] * GROUP, [SMEM, HBM], "near", 8,
            member, state.reshape(local, groups, GROUP, rows, width),
            scratch=(pltpu.SemaphoreType.DMA((GROUP,)),),
        )
        blocks = [
            lax.ppermute(block, "sector", [(i, i ^ k) for i in range(devices)]) if k else block
            for k, block in enumerate(blocks)
        ]

    spectrum = transform(forward, pieces, blocks[1:])
    if by_groups:
        state = call(
            far_kernel, shape((groups, GROUP * local, rows, width), BF16), [SMEM] + [ANY] * GROUP, "far", 8,
            member, *blocks, scratch=(pltpu.SemaphoreType.DMA((GROUP, local)),),
        )
    harmonic = exchange(spectrum.reshape(devices, 2, rows, width))

    if not aligned:
        harmonic = harmonic.transpose(1, 0, 2, 3).reshape(1, 2, cycle, width)
    faces = call(
        faces_kernel, shape((2, 2 * face, width), BF16), [VMEM, HBM], "faces", 8,
        sent, harmonic, scratch=fetch_scratch(harmonic),
    )
    if by_groups:
        members = [[GROUP * z + i for z in range(groups)] for i in range(GROUP)]
        state = lax.all_to_all(
            state, "sector", split_axis=0, concat_axis=0, tiled=True, axis_index_groups=members
        ).reshape(sectors, rows, width)
        state = call(
            stage_kernel, shape(state.shape, BF16), [HBM], "stage", 8, state,
            scratch=(pltpu.SemaphoreType.DMA((4,)),),
        )
    else:
        state = exchange(by_chunk(state, devices)).reshape(sectors, rows, width)
    own = call(
        own_kernel, shape((cycle, 2 * width), F32), [SMEM, VMEM, HBM], "own", 12, paired, weight, harmonic,
        scratch=fetch_scratch(harmonic),
    )
    if cycles == 2:
        near = lax.ppermute(faces, "radial", [(0, 1), (1, 0)])
    else:
        lower = step(faces, 1)
        upper = step(faces, -1)
        beyond_above = step(faces[:, :face], -2)
        beyond_below = step(faces[:, face:], 2)
        far_above = (upper[:, face:].astype(F32) + beyond_above.astype(F32)).astype(BF16)
        far_below = (lower[:, :face].astype(F32) + beyond_below.astype(F32)).astype(BF16)
        near = jnp.concatenate([lower[:, face:], upper[:, :face], far_above, far_below], axis=1)
    middle, leaving = call(
        middle_kernel,
        (shape((cycle, 2 * width), BF16), shape((edges, 2 * width), BF16)),
        [SMEM, VMEM, VMEM, VMEM, VMEM], "middle", 12,
        paired, own, edge, outward, near,
    )
    if cycles == 2:
        got = lax.ppermute(leaving, "radial", [(0, 1), (1, 0)])
    else:
        got = jnp.concatenate([step(leaving[:face], 1), step(leaving[face:], -1)], axis=0)
    back = call(
        back_kernel, shape((cycle, 2 * width), F32), [SMEM, VMEM, VMEM], "back", 12, paired, turned, middle
    )
    solved = call(
        finish_kernel, shape((devices, 2, rows, width) if aligned else (1, 2, cycle, width), BF16),
        [VMEM, VMEM, VMEM], "finish", 12, scattered, back, got,
    )
    if not aligned:
        solved = solved.reshape(2, devices, rows, width).transpose(1, 0, 2, 3)
    pieces = exchange(solved).reshape(sectors, rows, width)
    found = respond(inverse, pieces, state).reshape(devices, local, rows)
    return exchange(found).transpose(1, 0, 2).reshape(local, cycle)


def solution(mesh):
    return jax.shard_map(
        per_device,
        mesh=mesh,
        in_specs=(
            P("sector", "radial", None),
            P("sector", "radial", None),
            P("sector", None, "radial", None),
            P(),
            P("radial", None, None),
        ),
        out_specs=P("sector", "radial"),
        check_vma=False,
    )
```

```python
import math

import jax
import jax.numpy as jnp
from jax import lax
from jax.experimental import pallas as pl
from jax.experimental.pallas import tpu as pltpu
from jax.sharding import PartitionSpec as P

F32 = jnp.float32
BF16 = jnp.bfloat16
VMEM = pl.BlockSpec(memory_space=pltpu.VMEM)
SMEM = pl.BlockSpec(memory_space=pltpu.SMEM)
ANY = pl.BlockSpec(memory_space=pl.ANY)
HBM = pl.BlockSpec(memory_space=pltpu.HBM)
TILE = 16
TOKEN = jax.ShapeDtypeStruct((8, 128), jnp.float32)


def tables(assign, sectors):
    position = jnp.arange(sectors, dtype=jnp.int32)
    phases = assign[:, None] * position[None, :] % sectors
    angles = phases.astype(F32) * (2.0 * math.pi / sectors)
    paired = (assign == 0)[:, None]
    alternate = (1 - 2 * (position % 2)).astype(F32)[None, :]
    cos, sin = jnp.cos(angles), jnp.sin(angles)
    forward = jnp.stack([cos, jnp.where(paired, alternate, -sin)], axis=1)
    inverse = jnp.stack(
        [jnp.where(paired, 1.0, 2.0) * cos / sectors, jnp.where(paired, alternate, -2.0 * sin) / sectors],
        axis=1,
    )
    forward = forward.reshape(2 * assign.shape[0], sectors).astype(BF16)
    inverse = jnp.transpose(inverse.reshape(2 * assign.shape[0], sectors)).astype(BF16)
    return forward, inverse


def dot(a, b):
    return jnp.dot(a, b, preferred_element_type=F32)


def tiles(rows):
    return [slice(start, start + TILE) for start in range(0, rows, TILE)]


def transform_kernel(table_ref, x_ref, after_ref, out_ref):
    count, rows, width = x_ref.shape
    for span in tiles(rows):
        tile = x_ref[:, span, :].reshape(count * TILE, width)
        out_ref[:, span, :] = dot(table_ref[...], tile).astype(BF16).reshape(count, TILE, width)


def transform(table, pieces, after):
    rows = pieces.shape[1]
    if rows % TILE:
        return jnp.einsum("ks,sdr->kdr", table, pieces, preferred_element_type=F32).astype(BF16)
    return call(
        transform_kernel, jax.ShapeDtypeStruct(pieces.shape, BF16), [VMEM, VMEM, ANY], "transform", 8,
        table, pieces, after,
    )


def stage_kernel(x_ref, out_ref, sems):
    step = x_ref.shape[0] // sems.shape[0]
    copies = []
    for j in range(sems.shape[0]):
        span = slice(j * step, (j + 1) * step)
        copies.append(pltpu.make_async_copy(x_ref.at[span], out_ref.at[span], sems.at[j]))
        copies[-1].start()
    for copy in copies:
        copy.wait()


def respond_kernel(table_ref, x_ref, state_ref, out_ref):
    count, rows, width = x_ref.shape
    lanes = 128
    place = lax.broadcasted_iota(jnp.int32, (count * TILE, lanes), 0) % lanes
    diagonal = place == lax.broadcasted_iota(jnp.int32, (count * TILE, lanes), 1)
    for index, span in enumerate(tiles(rows)):
        tile = x_ref[:, span, :].reshape(count * TILE, width)
        adjoint = dot(table_ref[...], tile).astype(BF16).astype(F32)
        state = state_ref[:, span, :].reshape(count * TILE, width).astype(F32)
        total = jnp.sum(adjoint * state, axis=1, keepdims=True)
        total = jnp.where(diagonal, total, 0.0)
        out_ref[index] = jnp.sum(total.reshape(count * TILE // lanes, lanes, lanes), axis=1)


def respond(table, pieces, state):
    count, rows, _ = pieces.shape
    if rows % TILE:
        adjoint = jnp.einsum("sk,kdr->sdr", table, pieces, preferred_element_type=F32).astype(BF16)
        return jnp.sum(adjoint.astype(F32) * state.astype(F32), axis=-1)
    sums = call(
        respond_kernel, jax.ShapeDtypeStruct((rows // TILE, count * TILE // 128, 128), F32),
        [VMEM, VMEM, VMEM], "respond", 12, table, pieces, state,
    )
    return sums.reshape(rows // TILE, count, TILE).transpose(1, 0, 2).reshape(count, rows)


def rows_of(x_ref, part):
    chunks, _, rows, width = x_ref.shape
    return x_ref[:, part].reshape(chunks * rows, width)


def fetch(x_ref, held_ref, sems):
    chunks, pieces = x_ref.shape[0], sems.shape[0]
    step = chunks // pieces
    copies = []
    for j in range(pieces):
        span = slice(j * step, (j + 1) * step)
        copies.append(pltpu.make_async_copy(x_ref.at[span], held_ref.at[span], sems.at[j]))
        copies[-1].start()
    return copies


def fetch_scratch(array):
    return pltpu.VMEM(array.shape, array.dtype), pltpu.SemaphoreType.DMA((math.gcd(array.shape[0], 8),))


def faces_kernel(index_ref, x_ref, out_ref, held_ref, sems):
    copies = fetch(x_ref, held_ref, sems)
    chunks, _, rows, width = x_ref.shape
    count = index_ref.shape[1]
    square = (count, count)
    diagonal = lax.broadcasted_iota(jnp.int32, square, 0) == lax.broadcasted_iota(jnp.int32, square, 1)
    column = jnp.sum(jnp.where(diagonal, index_ref[...].astype(F32), 0.0), axis=1, keepdims=True)
    pick = column.astype(jnp.int32) == lax.broadcasted_iota(jnp.int32, (count, chunks * rows), 1)
    pick = jnp.where(pick, 1.0, 0.0).astype(BF16)
    for copy in copies:
        copy.wait()
    for part in range(2):
        out_ref[part] = dot(pick, rows_of(held_ref, part)).astype(BF16)


def widen(table):
    count = table.shape[0]
    side = count * TILE
    spread = lax.broadcasted_iota(jnp.int32, (side, count), 0) // TILE
    spread = spread == lax.broadcasted_iota(jnp.int32, (side, count), 1)
    spread = jnp.where(spread, 1.0, 0.0).astype(BF16)
    tall = dot(spread, table).astype(BF16)
    full = lax.dot_general(tall, spread, (((1,), (1,)), ((), ())), preferred_element_type=F32)
    row = lax.broadcasted_iota(jnp.int32, (side, side), 0) % TILE
    column = lax.broadcasted_iota(jnp.int32, (side, side), 1) % TILE
    return jnp.where(row == column, full, 0.0).astype(BF16)


def widen_kernel(forward_ref, inverse_ref, forward_out, inverse_out):
    forward_out[...] = widen(forward_ref[...])
    inverse_out[...] = widen(inverse_ref[...])


def prepare_kernel(low_ref, index_ref, weight_ref, edge_ref, turned_ref, away_ref):
    cycle = weight_ref.shape[1]
    count = index_ref.shape[1]
    leaving = away_ref.shape[1]
    face = (weight_ref.shape[2] - cycle) // 2
    pick = lax.broadcasted_iota(jnp.int32, (cycle, count), 0) == index_ref[...]
    pick = jnp.where(pick, 1.0, 0.0).astype(BF16)
    for part in range(2):
        own = weight_ref[part, :, :cycle]
        outward = weight_ref[part, :, cycle:]
        if leaving == face:
            outward = jnp.where(low_ref[0] != 0, outward[:, :face], outward[:, face:])
        edge_ref[part, :, :count] = dot(own, pick).astype(BF16)
        edge_ref[part, :, count:] = outward
        turned_ref[part] = own.T
        away_ref[part] = outward.T


def chunk_kernel(x_ref, out_ref, token_ref, sems):
    token_ref[...] = jnp.zeros_like(token_ref)
    local, devices = x_ref.shape[:2]
    count = sems.shape[0]
    step = devices // count
    copies = []
    for j in range(count):
        span = slice(j * step, (j + 1) * step)
        for i in range(local):
            copies.append(pltpu.make_async_copy(x_ref.at[i, span], out_ref.at[span, i], sems.at[j, i]))
            copies[-1].start()
    for copy in copies:
        copy.wait()


def by_chunk(block, devices):
    local, cycle, width = block.shape
    rows = cycle // devices
    split = block.reshape(local, devices, rows, width)
    if rows % TILE or devices % 4:
        return split.transpose(1, 0, 2, 3), None
    out = jax.ShapeDtypeStruct((devices, local, rows, width), block.dtype)
    return call(
        chunk_kernel, (out, TOKEN), [HBM], "chunk", 8, split,
        scratch=(pltpu.SemaphoreType.DMA((4, local)),),
    )


def right_sides(real, imag, paired):
    zero = jnp.zeros_like(imag)
    turned = jnp.where(paired, zero, imag)
    upper = jnp.concatenate([real, turned], axis=1)
    lower = jnp.concatenate([-turned, jnp.where(paired, imag, real)], axis=1)
    return upper, lower


def own_kernel(paired_ref, weight_ref, x_ref, out_ref, held_ref, sems):
    cycle = weight_ref.shape[1]
    for copy in fetch(x_ref, held_ref, sems):
        copy.wait()
    upper, lower = right_sides(rows_of(held_ref, 0), rows_of(held_ref, 1), paired_ref[0] != 0)
    out_ref[...] = dot(weight_ref[0, :, :cycle], upper) + dot(weight_ref[1, :, :cycle], lower)


def back_sides(real, imag, paired):
    zero = jnp.zeros_like(imag)
    turned = jnp.where(paired, zero, imag)
    upper = jnp.concatenate([real, turned], axis=1)
    lower = jnp.concatenate([turned, jnp.where(paired, imag, -real)], axis=1)
    return upper, lower


def middle_kernel(paired_ref, own_ref, edge_ref, back_ref, near_ref, middle_ref, out_ref):
    paired = paired_ref[0] != 0
    width = near_ref.shape[2]
    upper, lower = right_sides(near_ref[0], near_ref[1], paired)
    middle = own_ref[...] + dot(edge_ref[0], upper) + dot(edge_ref[1], lower)
    middle = middle.astype(BF16)
    middle_ref[...] = middle
    upper, lower = back_sides(middle[:, :width], middle[:, width:], paired)
    out_ref[...] = (dot(back_ref[0], upper) + dot(back_ref[1], lower)).astype(BF16)


def back_kernel(paired_ref, turned_ref, middle_ref, out_ref):
    paired = paired_ref[0] != 0
    width = middle_ref.shape[1] // 2
    upper, lower = back_sides(middle_ref[:, :width], middle_ref[:, width:], paired)
    out_ref[...] = dot(turned_ref[0], upper) + dot(turned_ref[1], lower)


def finish_kernel(index_ref, back_ref, got_ref, out_ref):
    chunks, _, rows, width = out_ref.shape
    cycle = back_ref.shape[0]
    count = index_ref.shape[1]
    pick = lax.broadcasted_iota(jnp.int32, (cycle, count), 0) == index_ref[...]
    pick = jnp.where(pick, 1.0, 0.0).astype(BF16)
    total = (back_ref[...] + dot(pick, got_ref[...])).astype(BF16)
    for part in range(2):
        out_ref[:, part] = total[:, part * width : (part + 1) * width].reshape(chunks, rows, width)


def placed(operand, spec):
    space = spec.memory_space
    return pltpu.with_memory_space_constraint(operand, space) if space in (pltpu.VMEM, pltpu.HBM) else operand


def call(kernel, outs, specs, name, mebibytes, *operands, scratch=(), out_spaces=None):
    single = not isinstance(outs, (list, tuple))
    shapes = [outs] if single else list(outs)
    spaces = out_spaces or [pltpu.VMEM] * len(shapes)
    results = pl.pallas_call(
        kernel,
        out_shape=[space(out.shape, out.dtype) for out, space in zip(shapes, spaces)],
        in_specs=specs,
        out_specs=[pl.BlockSpec(memory_space=space) for space in spaces],
        scratch_shapes=scratch,
        compiler_params=pltpu.CompilerParams(vmem_limit_bytes=mebibytes * 1024 * 1024),
        name=name,
    )(*(placed(operand, spec) for operand, spec in zip(operands, specs)))
    return results[0] if single else list(results)


def per_device(loads, state, factors, assign, iface):
    local, cycle, width = loads.shape
    inner, outer = iface[0, 0], iface[0, 1]
    face = inner.shape[0]
    devices = lax.axis_size("sector")
    cycles = lax.axis_size("radial")
    here = lax.axis_index("radial")
    sectors = local * devices
    rows = cycle // devices
    aligned = rows % TILE == 0
    weight = factors[0]
    forward, inverse = tables(assign, sectors)
    paired = (assign[lax.axis_index("sector")] == 0).astype(jnp.int32).reshape(1)
    shape = jax.ShapeDtypeStruct

    def exchange(pieces):
        return lax.all_to_all(pieces, "sector", split_axis=0, concat_axis=0, tiled=True)

    def step(block, shift):
        pairs = [(i, i + shift) for i in range(cycles) if 0 <= i + shift < cycles]
        return lax.ppermute(block, "radial", pairs)

    if cycles == 2:
        toward = jnp.where(here == 0, outer, inner)
        away = jnp.where(here == 0, inner, outer)
        sent = jnp.concatenate([toward, away])
        gathered, scattered = toward, away
    else:
        sent = gathered = jnp.concatenate([inner, outer])
        scattered = jnp.concatenate([outer, inner])
    sent = sent.reshape(1, -1)
    scattered = scattered.reshape(1, -1)
    edges = gathered.shape[0]

    pieces = exchange(by_chunk(loads, devices)[0]).reshape(sectors, rows, width)

    edge, turned, outward = call(
        prepare_kernel,
        (shape((2, cycle, 2 * edges), BF16), shape((2, cycle, cycle), BF16), shape((2, edges, cycle), BF16)),
        [SMEM, VMEM, VMEM], "prepare", 20,
        (here == 0).astype(jnp.int32).reshape(1), gathered.reshape(1, -1), weight,
    )
    if aligned:
        wide = shape((sectors * TILE, sectors * TILE), BF16)
        forward, inverse = call(widen_kernel, (wide, wide), [VMEM, VMEM], "widen", 12, forward, inverse)
    state, token = by_chunk(state, devices)
    spectrum = transform(forward, pieces, token)
    harmonic = exchange(spectrum.reshape(devices, 2, rows, width))
    state = exchange(state).reshape(sectors, rows, width)
    if aligned:
        state = call(
            stage_kernel, shape(state.shape, BF16), [HBM], "stage", 8, state,
            scratch=(pltpu.SemaphoreType.DMA((4,)),),
        )

    if not aligned:
        harmonic = harmonic.transpose(1, 0, 2, 3).reshape(1, 2, cycle, width)
    faces = call(
        faces_kernel, shape((2, 2 * face, width), BF16), [VMEM, HBM], "faces", 8,
        sent, harmonic, scratch=fetch_scratch(harmonic),
    )
    own = call(
        own_kernel, shape((cycle, 2 * width), F32), [SMEM, VMEM, HBM], "own", 12, paired, weight, harmonic,
        scratch=fetch_scratch(harmonic),
    )
    if cycles == 2:
        near = lax.ppermute(faces, "radial", [(0, 1), (1, 0)])
    else:
        lower = step(faces, 1)
        upper = step(faces, -1)
        beyond_above = step(faces[:, :face], -2)
        beyond_below = step(faces[:, face:], 2)
        far_above = (upper[:, face:].astype(F32) + beyond_above.astype(F32)).astype(BF16)
        far_below = (lower[:, :face].astype(F32) + beyond_below.astype(F32)).astype(BF16)
        near = jnp.concatenate([lower[:, face:], upper[:, :face], far_above, far_below], axis=1)
    middle, leaving = call(
        middle_kernel,
        (shape((cycle, 2 * width), BF16), shape((edges, 2 * width), BF16)),
        [SMEM, VMEM, VMEM, VMEM, VMEM], "middle", 12,
        paired, own, edge, outward, near,
    )
    if cycles == 2:
        got = lax.ppermute(leaving, "radial", [(0, 1), (1, 0)])
    else:
        got = jnp.concatenate([step(leaving[:face], 1), step(leaving[face:], -1)], axis=0)
    back = call(
        back_kernel, shape((cycle, 2 * width), F32), [SMEM, VMEM, VMEM], "back", 12, paired, turned, middle
    )
    solved = call(
        finish_kernel, shape((devices, 2, rows, width) if aligned else (1, 2, cycle, width), BF16),
        [VMEM, VMEM, VMEM], "finish", 12, scattered, back, got,
    )
    if not aligned:
        solved = solved.reshape(2, devices, rows, width).transpose(1, 0, 2, 3)
    pieces = exchange(solved).reshape(sectors, rows, width)
    found = respond(inverse, pieces, state).reshape(devices, local, rows)
    return exchange(found).transpose(1, 0, 2).reshape(local, cycle)


def solution(mesh):
    return jax.shard_map(
        per_device,
        mesh=mesh,
        in_specs=(
            P("sector", "radial", None),
            P("sector", "radial", None),
            P("sector", None, "radial", None),
            P(),
            P("radial", None, None),
        ),
        out_specs=P("sector", "radial"),
        check_vma=False,
    )
```

```python
import math

import jax
import jax.numpy as jnp
from jax import lax
from jax.experimental import pallas as pl
from jax.experimental.pallas import tpu as pltpu
from jax.sharding import PartitionSpec as P

F32 = jnp.float32
BF16 = jnp.bfloat16
VMEM = pl.BlockSpec(memory_space=pltpu.VMEM)
SMEM = pl.BlockSpec(memory_space=pltpu.SMEM)
ANY = pl.BlockSpec(memory_space=pl.ANY)
HBM = pl.BlockSpec(memory_space=pltpu.HBM)
TILE = 16
TOKEN = jax.ShapeDtypeStruct((8, 128), jnp.float32)


def tables(assign, sectors):
    position = jnp.arange(sectors, dtype=jnp.int32)
    phases = assign[:, None] * position[None, :] % sectors
    angles = phases.astype(F32) * (2.0 * math.pi / sectors)
    paired = (assign == 0)[:, None]
    alternate = (1 - 2 * (position % 2)).astype(F32)[None, :]
    cos, sin = jnp.cos(angles), jnp.sin(angles)
    forward = jnp.stack([cos, jnp.where(paired, alternate, -sin)], axis=1)
    inverse = jnp.stack(
        [jnp.where(paired, 1.0, 2.0) * cos / sectors, jnp.where(paired, alternate, -2.0 * sin) / sectors],
        axis=1,
    )
    forward = forward.reshape(2 * assign.shape[0], sectors).astype(BF16)
    inverse = jnp.transpose(inverse.reshape(2 * assign.shape[0], sectors)).astype(BF16)
    return forward, inverse


def dot(a, b):
    return jnp.dot(a, b, preferred_element_type=F32)


def tiles(rows):
    return [slice(start, start + TILE) for start in range(0, rows, TILE)]


def transform_kernel(table_ref, x_ref, after_ref, out_ref):
    count, rows, width = x_ref.shape
    for span in tiles(rows):
        tile = x_ref[:, span, :].reshape(count * TILE, width)
        out_ref[:, span, :] = dot(table_ref[...], tile).astype(BF16).reshape(count, TILE, width)


def transform(table, pieces, after):
    rows = pieces.shape[1]
    if rows % TILE:
        return jnp.einsum("ks,sdr->kdr", table, pieces, preferred_element_type=F32).astype(BF16)
    return call(
        transform_kernel, jax.ShapeDtypeStruct(pieces.shape, BF16), [VMEM, VMEM, ANY], "transform", 8,
        table, pieces, after,
    )


def stage_kernel(x_ref, out_ref, sems):
    step = x_ref.shape[0] // sems.shape[0]
    copies = []
    for j in range(sems.shape[0]):
        span = slice(j * step, (j + 1) * step)
        copies.append(pltpu.make_async_copy(x_ref.at[span], out_ref.at[span], sems.at[j]))
        copies[-1].start()
    for copy in copies:
        copy.wait()


def respond_kernel(table_ref, x_ref, state_ref, out_ref):
    count, rows, width = x_ref.shape
    lanes = 128
    place = lax.broadcasted_iota(jnp.int32, (count * TILE, lanes), 0) % lanes
    diagonal = place == lax.broadcasted_iota(jnp.int32, (count * TILE, lanes), 1)
    for index, span in enumerate(tiles(rows)):
        tile = x_ref[:, span, :].reshape(count * TILE, width)
        adjoint = dot(table_ref[...], tile).astype(BF16).astype(F32)
        state = state_ref[:, span, :].reshape(count * TILE, width).astype(F32)
        total = jnp.sum(adjoint * state, axis=1, keepdims=True)
        total = jnp.where(diagonal, total, 0.0)
        out_ref[index] = jnp.sum(total.reshape(count * TILE // lanes, lanes, lanes), axis=1)


def respond(table, pieces, state):
    count, rows, _ = pieces.shape
    if rows % TILE:
        adjoint = jnp.einsum("sk,kdr->sdr", table, pieces, preferred_element_type=F32).astype(BF16)
        return jnp.sum(adjoint.astype(F32) * state.astype(F32), axis=-1)
    sums = call(
        respond_kernel, jax.ShapeDtypeStruct((rows // TILE, count * TILE // 128, 128), F32),
        [VMEM, VMEM, VMEM], "respond", 12, table, pieces, state,
    )
    return sums.reshape(rows // TILE, count, TILE).transpose(1, 0, 2).reshape(count, rows)


def rows_of(x_ref, part):
    chunks, _, rows, width = x_ref.shape
    return x_ref[:, part].reshape(chunks * rows, width)


def fetch(x_ref, held_ref, sems):
    chunks, pieces = x_ref.shape[0], sems.shape[0]
    step = chunks // pieces
    copies = []
    for j in range(pieces):
        span = slice(j * step, (j + 1) * step)
        copies.append(pltpu.make_async_copy(x_ref.at[span], held_ref.at[span], sems.at[j]))
        copies[-1].start()
    return copies


def fetch_scratch(array):
    return pltpu.VMEM(array.shape, array.dtype), pltpu.SemaphoreType.DMA((math.gcd(array.shape[0], 8),))


def faces_kernel(index_ref, x_ref, out_ref, held_ref, sems):
    copies = fetch(x_ref, held_ref, sems)
    chunks, _, rows, width = x_ref.shape
    count = index_ref.shape[1]
    square = (count, count)
    diagonal = lax.broadcasted_iota(jnp.int32, square, 0) == lax.broadcasted_iota(jnp.int32, square, 1)
    column = jnp.sum(jnp.where(diagonal, index_ref[...].astype(F32), 0.0), axis=1, keepdims=True)
    pick = column.astype(jnp.int32) == lax.broadcasted_iota(jnp.int32, (count, chunks * rows), 1)
    pick = jnp.where(pick, 1.0, 0.0).astype(BF16)
    for copy in copies:
        copy.wait()
    for part in range(2):
        out_ref[part] = dot(pick, rows_of(held_ref, part)).astype(BF16)


def widen(table):
    count = table.shape[0]
    side = count * TILE
    spread = lax.broadcasted_iota(jnp.int32, (side, count), 0) // TILE
    spread = spread == lax.broadcasted_iota(jnp.int32, (side, count), 1)
    spread = jnp.where(spread, 1.0, 0.0).astype(BF16)
    tall = dot(spread, table).astype(BF16)
    full = lax.dot_general(tall, spread, (((1,), (1,)), ((), ())), preferred_element_type=F32)
    row = lax.broadcasted_iota(jnp.int32, (side, side), 0) % TILE
    column = lax.broadcasted_iota(jnp.int32, (side, side), 1) % TILE
    return jnp.where(row == column, full, 0.0).astype(BF16)


def widen_kernel(forward_ref, inverse_ref, forward_out, inverse_out):
    forward_out[...] = widen(forward_ref[...])
    inverse_out[...] = widen(inverse_ref[...])


def prepare_kernel(low_ref, index_ref, weight_ref, edge_ref, turned_ref, away_ref):
    cycle = weight_ref.shape[1]
    count = index_ref.shape[1]
    leaving = away_ref.shape[1]
    face = (weight_ref.shape[2] - cycle) // 2
    pick = lax.broadcasted_iota(jnp.int32, (cycle, count), 0) == index_ref[...]
    pick = jnp.where(pick, 1.0, 0.0).astype(BF16)
    for part in range(2):
        own = weight_ref[part, :, :cycle]
        outward = weight_ref[part, :, cycle:]
        if leaving == face:
            outward = jnp.where(low_ref[0] != 0, outward[:, :face], outward[:, face:])
        edge_ref[part, :, :count] = dot(own, pick).astype(BF16)
        edge_ref[part, :, count:] = outward
        turned_ref[part] = own.T
        away_ref[part] = outward.T


def chunk_kernel(x_ref, out_ref, token_ref, sems):
    token_ref[...] = jnp.zeros_like(token_ref)
    local, devices = x_ref.shape[:2]
    count = sems.shape[0]
    step = devices // count
    copies = []
    for j in range(count):
        span = slice(j * step, (j + 1) * step)
        for i in range(local):
            copies.append(pltpu.make_async_copy(x_ref.at[i, span], out_ref.at[span, i], sems.at[j, i]))
            copies[-1].start()
    for copy in copies:
        copy.wait()


def by_chunk(block, devices):
    local, cycle, width = block.shape
    rows = cycle // devices
    split = block.reshape(local, devices, rows, width)
    if rows % TILE or devices % 4:
        return split.transpose(1, 0, 2, 3), None
    out = jax.ShapeDtypeStruct((devices, local, rows, width), block.dtype)
    return call(
        chunk_kernel, (out, TOKEN), [HBM], "chunk", 8, split,
        scratch=(pltpu.SemaphoreType.DMA((1, local)),),
    )


def right_sides(real, imag, paired):
    zero = jnp.zeros_like(imag)
    turned = jnp.where(paired, zero, imag)
    upper = jnp.concatenate([real, turned], axis=1)
    lower = jnp.concatenate([-turned, jnp.where(paired, imag, real)], axis=1)
    return upper, lower


def own_kernel(paired_ref, weight_ref, x_ref, out_ref, held_ref, sems):
    cycle = weight_ref.shape[1]
    for copy in fetch(x_ref, held_ref, sems):
        copy.wait()
    upper, lower = right_sides(rows_of(held_ref, 0), rows_of(held_ref, 1), paired_ref[0] != 0)
    out_ref[...] = dot(weight_ref[0, :, :cycle], upper) + dot(weight_ref[1, :, :cycle], lower)


def back_sides(real, imag, paired):
    zero = jnp.zeros_like(imag)
    turned = jnp.where(paired, zero, imag)
    upper = jnp.concatenate([real, turned], axis=1)
    lower = jnp.concatenate([turned, jnp.where(paired, imag, -real)], axis=1)
    return upper, lower


def middle_kernel(paired_ref, own_ref, edge_ref, back_ref, near_ref, middle_ref, out_ref):
    paired = paired_ref[0] != 0
    width = near_ref.shape[2]
    upper, lower = right_sides(near_ref[0], near_ref[1], paired)
    middle = own_ref[...] + dot(edge_ref[0], upper) + dot(edge_ref[1], lower)
    middle = middle.astype(BF16)
    middle_ref[...] = middle
    upper, lower = back_sides(middle[:, :width], middle[:, width:], paired)
    out_ref[...] = (dot(back_ref[0], upper) + dot(back_ref[1], lower)).astype(BF16)


def back_kernel(paired_ref, turned_ref, middle_ref, out_ref):
    paired = paired_ref[0] != 0
    width = middle_ref.shape[1] // 2
    upper, lower = back_sides(middle_ref[:, :width], middle_ref[:, width:], paired)
    out_ref[...] = dot(turned_ref[0], upper) + dot(turned_ref[1], lower)


def finish_kernel(index_ref, back_ref, got_ref, out_ref):
    chunks, _, rows, width = out_ref.shape
    cycle = back_ref.shape[0]
    count = index_ref.shape[1]
    pick = lax.broadcasted_iota(jnp.int32, (cycle, count), 0) == index_ref[...]
    pick = jnp.where(pick, 1.0, 0.0).astype(BF16)
    total = (back_ref[...] + dot(pick, got_ref[...])).astype(BF16)
    for part in range(2):
        out_ref[:, part] = total[:, part * width : (part + 1) * width].reshape(chunks, rows, width)


def placed(operand, spec):
    space = spec.memory_space
    return pltpu.with_memory_space_constraint(operand, space) if space in (pltpu.VMEM, pltpu.HBM) else operand


def call(kernel, outs, specs, name, mebibytes, *operands, scratch=(), out_spaces=None):
    single = not isinstance(outs, (list, tuple))
    shapes = [outs] if single else list(outs)
    spaces = out_spaces or [pltpu.VMEM] * len(shapes)
    results = pl.pallas_call(
        kernel,
        out_shape=[space(out.shape, out.dtype) for out, space in zip(shapes, spaces)],
        in_specs=specs,
        out_specs=[pl.BlockSpec(memory_space=space) for space in spaces],
        scratch_shapes=scratch,
        compiler_params=pltpu.CompilerParams(vmem_limit_bytes=mebibytes * 1024 * 1024),
        name=name,
    )(*(placed(operand, spec) for operand, spec in zip(operands, specs)))
    return results[0] if single else list(results)


def per_device(loads, state, factors, assign, iface):
    local, cycle, width = loads.shape
    inner, outer = iface[0, 0], iface[0, 1]
    face = inner.shape[0]
    devices = lax.axis_size("sector")
    cycles = lax.axis_size("radial")
    here = lax.axis_index("radial")
    sectors = local * devices
    rows = cycle // devices
    aligned = rows % TILE == 0
    weight = factors[0]
    forward, inverse = tables(assign, sectors)
    paired = (assign[lax.axis_index("sector")] == 0).astype(jnp.int32).reshape(1)
    shape = jax.ShapeDtypeStruct

    def exchange(pieces):
        return lax.all_to_all(pieces, "sector", split_axis=0, concat_axis=0, tiled=True)

    def step(block, shift):
        pairs = [(i, i + shift) for i in range(cycles) if 0 <= i + shift < cycles]
        return lax.ppermute(block, "radial", pairs)

    if cycles == 2:
        toward = jnp.where(here == 0, outer, inner)
        away = jnp.where(here == 0, inner, outer)
        sent = jnp.concatenate([toward, away])
        gathered, scattered = toward, away
    else:
        sent = gathered = jnp.concatenate([inner, outer])
        scattered = jnp.concatenate([outer, inner])
    sent = sent.reshape(1, -1)
    scattered = scattered.reshape(1, -1)
    edges = gathered.shape[0]

    pieces = exchange(by_chunk(loads, devices)[0]).reshape(sectors, rows, width)

    edge, turned, outward = call(
        prepare_kernel,
        (shape((2, cycle, 2 * edges), BF16), shape((2, cycle, cycle), BF16), shape((2, edges, cycle), BF16)),
        [SMEM, VMEM, VMEM], "prepare", 20,
        (here == 0).astype(jnp.int32).reshape(1), gathered.reshape(1, -1), weight,
    )
    if aligned:
        wide = shape((sectors * TILE, sectors * TILE), BF16)
        forward, inverse = call(widen_kernel, (wide, wide), [VMEM, VMEM], "widen", 12, forward, inverse)
    state, token = by_chunk(state, devices)
    spectrum = transform(forward, pieces, token)
    harmonic = exchange(spectrum.reshape(devices, 2, rows, width))
    state = exchange(state).reshape(sectors, rows, width)
    if aligned:
        state = call(
            stage_kernel, shape(state.shape, BF16), [HBM], "stage", 8, state,
            scratch=(pltpu.SemaphoreType.DMA((4,)),),
        )

    if not aligned:
        harmonic = harmonic.transpose(1, 0, 2, 3).reshape(1, 2, cycle, width)
    faces = call(
        faces_kernel, shape((2, 2 * face, width), BF16), [VMEM, HBM], "faces", 8,
        sent, harmonic, scratch=fetch_scratch(harmonic),
    )
    own = call(
        own_kernel, shape((cycle, 2 * width), F32), [SMEM, VMEM, HBM], "own", 12, paired, weight, harmonic,
        scratch=fetch_scratch(harmonic),
    )
    if cycles == 2:
        near = lax.ppermute(faces, "radial", [(0, 1), (1, 0)])
    else:
        lower = step(faces, 1)
        upper = step(faces, -1)
        beyond_above = step(faces[:, :face], -2)
        beyond_below = step(faces[:, face:], 2)
        far_above = (upper[:, face:].astype(F32) + beyond_above.astype(F32)).astype(BF16)
        far_below = (lower[:, :face].astype(F32) + beyond_below.astype(F32)).astype(BF16)
        near = jnp.concatenate([lower[:, face:], upper[:, :face], far_above, far_below], axis=1)
    middle, leaving = call(
        middle_kernel,
        (shape((cycle, 2 * width), BF16), shape((edges, 2 * width), BF16)),
        [SMEM, VMEM, VMEM, VMEM, VMEM], "middle", 12,
        paired, own, edge, outward, near,
    )
    if cycles == 2:
        got = lax.ppermute(leaving, "radial", [(0, 1), (1, 0)])
    else:
        got = jnp.concatenate([step(leaving[:face], 1), step(leaving[face:], -1)], axis=0)
    back = call(
        back_kernel, shape((cycle, 2 * width), F32), [SMEM, VMEM, VMEM], "back", 12, paired, turned, middle
    )
    solved = call(
        finish_kernel, shape((devices, 2, rows, width) if aligned else (1, 2, cycle, width), BF16),
        [VMEM, VMEM, VMEM], "finish", 12, scattered, back, got,
    )
    if not aligned:
        solved = solved.reshape(2, devices, rows, width).transpose(1, 0, 2, 3)
    pieces = exchange(solved).reshape(sectors, rows, width)
    found = respond(inverse, pieces, state).reshape(devices, local, rows)
    return exchange(found).transpose(1, 0, 2).reshape(local, cycle)


def solution(mesh):
    return jax.shard_map(
        per_device,
        mesh=mesh,
        in_specs=(
            P("sector", "radial", None),
            P("sector", "radial", None),
            P("sector", None, "radial", None),
            P(),
            P("radial", None, None),
        ),
        out_specs=P("sector", "radial"),
        check_vma=False,
    )
```

```python
import math

import jax
import jax.numpy as jnp
from jax import lax
from jax.experimental import pallas as pl
from jax.experimental.pallas import tpu as pltpu
from jax.sharding import PartitionSpec as P

F32 = jnp.float32
BF16 = jnp.bfloat16
VMEM = pl.BlockSpec(memory_space=pltpu.VMEM)
SMEM = pl.BlockSpec(memory_space=pltpu.SMEM)
ANY = pl.BlockSpec(memory_space=pl.ANY)
HBM = pl.BlockSpec(memory_space=pltpu.HBM)
TILE = 16
TOKEN = jax.ShapeDtypeStruct((8, 128), jnp.float32)


def tables(assign, sectors):
    position = jnp.arange(sectors, dtype=jnp.int32)
    phases = assign[:, None] * position[None, :] % sectors
    angles = phases.astype(F32) * (2.0 * math.pi / sectors)
    paired = (assign == 0)[:, None]
    alternate = (1 - 2 * (position % 2)).astype(F32)[None, :]
    cos, sin = jnp.cos(angles), jnp.sin(angles)
    forward = jnp.stack([cos, jnp.where(paired, alternate, -sin)], axis=1)
    inverse = jnp.stack(
        [jnp.where(paired, 1.0, 2.0) * cos / sectors, jnp.where(paired, alternate, -2.0 * sin) / sectors],
        axis=1,
    )
    forward = forward.reshape(2 * assign.shape[0], sectors).astype(BF16)
    inverse = jnp.transpose(inverse.reshape(2 * assign.shape[0], sectors)).astype(BF16)
    return forward, inverse


def dot(a, b):
    return jnp.dot(a, b, preferred_element_type=F32)


def tiles(rows):
    return [slice(start, start + TILE) for start in range(0, rows, TILE)]


def transform_kernel(table_ref, x_ref, after_ref, out_ref):
    count, rows, width = x_ref.shape
    for span in tiles(rows):
        tile = x_ref[:, span, :].reshape(count * TILE, width)
        out_ref[:, span, :] = dot(table_ref[...], tile).astype(BF16).reshape(count, TILE, width)


def transform(table, pieces, after):
    rows = pieces.shape[1]
    if rows % TILE:
        return jnp.einsum("ks,sdr->kdr", table, pieces, preferred_element_type=F32).astype(BF16)
    return call(
        transform_kernel, jax.ShapeDtypeStruct(pieces.shape, BF16), [VMEM, VMEM, ANY], "transform", 8,
        table, pieces, after,
    )


def stage_kernel(x_ref, out_ref, sems):
    step = x_ref.shape[0] // sems.shape[0]
    copies = []
    for j in range(sems.shape[0]):
        span = slice(j * step, (j + 1) * step)
        copies.append(pltpu.make_async_copy(x_ref.at[span], out_ref.at[span], sems.at[j]))
        copies[-1].start()
    for copy in copies:
        copy.wait()


def respond_kernel(table_ref, x_ref, state_ref, out_ref):
    count, rows, width = x_ref.shape
    lanes = 128
    place = lax.broadcasted_iota(jnp.int32, (count * TILE, lanes), 0) % lanes
    diagonal = place == lax.broadcasted_iota(jnp.int32, (count * TILE, lanes), 1)
    for index, span in enumerate(tiles(rows)):
        tile = x_ref[:, span, :].reshape(count * TILE, width)
        adjoint = dot(table_ref[...], tile).astype(BF16).astype(F32)
        state = state_ref[:, span, :].reshape(count * TILE, width).astype(F32)
        total = jnp.sum(adjoint * state, axis=1, keepdims=True)
        total = jnp.where(diagonal, total, 0.0)
        out_ref[index] = jnp.sum(total.reshape(count * TILE // lanes, lanes, lanes), axis=1)


def respond(table, pieces, state):
    count, rows, _ = pieces.shape
    if rows % TILE:
        adjoint = jnp.einsum("sk,kdr->sdr", table, pieces, preferred_element_type=F32).astype(BF16)
        return jnp.sum(adjoint.astype(F32) * state.astype(F32), axis=-1)
    sums = call(
        respond_kernel, jax.ShapeDtypeStruct((rows // TILE, count * TILE // 128, 128), F32),
        [VMEM, VMEM, VMEM], "respond", 12, table, pieces, state,
    )
    return sums.reshape(rows // TILE, count, TILE).transpose(1, 0, 2).reshape(count, rows)


def rows_of(x_ref, part):
    chunks, _, rows, width = x_ref.shape
    return x_ref[:, part].reshape(chunks * rows, width)


def fetch(x_ref, held_ref, sems):
    chunks, pieces = x_ref.shape[0], sems.shape[0]
    step = chunks // pieces
    copies = []
    for j in range(pieces):
        span = slice(j * step, (j + 1) * step)
        copies.append(pltpu.make_async_copy(x_ref.at[span], held_ref.at[span], sems.at[j]))
        copies[-1].start()
    return copies


def fetch_scratch(array):
    return pltpu.VMEM(array.shape, array.dtype), pltpu.SemaphoreType.DMA((math.gcd(array.shape[0], 8),))


def faces_kernel(index_ref, x_ref, out_ref):
    chunks, _, rows, width = x_ref.shape
    count = index_ref.shape[1]
    square = (count, count)
    diagonal = lax.broadcasted_iota(jnp.int32, square, 0) == lax.broadcasted_iota(jnp.int32, square, 1)
    column = jnp.sum(jnp.where(diagonal, index_ref[...].astype(F32), 0.0), axis=1, keepdims=True)
    pick = column.astype(jnp.int32) == lax.broadcasted_iota(jnp.int32, (count, chunks * rows), 1)
    pick = jnp.where(pick, 1.0, 0.0).astype(BF16)
    for part in range(2):
        out_ref[part] = dot(pick, rows_of(x_ref, part)).astype(BF16)


def widen(table):
    count = table.shape[0]
    side = count * TILE
    spread = lax.broadcasted_iota(jnp.int32, (side, count), 0) // TILE
    spread = spread == lax.broadcasted_iota(jnp.int32, (side, count), 1)
    spread = jnp.where(spread, 1.0, 0.0).astype(BF16)
    tall = dot(spread, table).astype(BF16)
    full = lax.dot_general(tall, spread, (((1,), (1,)), ((), ())), preferred_element_type=F32)
    row = lax.broadcasted_iota(jnp.int32, (side, side), 0) % TILE
    column = lax.broadcasted_iota(jnp.int32, (side, side), 1) % TILE
    return jnp.where(row == column, full, 0.0).astype(BF16)


def widen_kernel(forward_ref, inverse_ref, forward_out, inverse_out):
    forward_out[...] = widen(forward_ref[...])
    inverse_out[...] = widen(inverse_ref[...])


def prepare_kernel(low_ref, index_ref, weight_ref, edge_ref, turned_ref, away_ref):
    cycle = weight_ref.shape[1]
    count = index_ref.shape[1]
    leaving = away_ref.shape[1]
    face = (weight_ref.shape[2] - cycle) // 2
    pick = lax.broadcasted_iota(jnp.int32, (cycle, count), 0) == index_ref[...]
    pick = jnp.where(pick, 1.0, 0.0).astype(BF16)
    for part in range(2):
        own = weight_ref[part, :, :cycle]
        outward = weight_ref[part, :, cycle:]
        if leaving == face:
            outward = jnp.where(low_ref[0] != 0, outward[:, :face], outward[:, face:])
        edge_ref[part, :, :count] = dot(own, pick).astype(BF16)
        edge_ref[part, :, count:] = outward
        turned_ref[part] = own.T
        away_ref[part] = outward.T


def chunk_kernel(x_ref, out_ref, token_ref, sems):
    token_ref[...] = jnp.zeros_like(token_ref)
    local, devices = x_ref.shape[:2]
    count = sems.shape[0]
    step = devices // count
    copies = []
    for j in range(count):
        span = slice(j * step, (j + 1) * step)
        for i in range(local):
            copies.append(pltpu.make_async_copy(x_ref.at[i, span], out_ref.at[span, i], sems.at[j, i]))
            copies[-1].start()
    for copy in copies:
        copy.wait()


def by_chunk(block, devices):
    local, cycle, width = block.shape
    rows = cycle // devices
    split = block.reshape(local, devices, rows, width)
    if rows % TILE or devices % 4:
        return split.transpose(1, 0, 2, 3), None
    out = jax.ShapeDtypeStruct((devices, local, rows, width), block.dtype)
    return call(
        chunk_kernel, (out, TOKEN), [HBM], "chunk", 8, split,
        scratch=(pltpu.SemaphoreType.DMA((1, local)),),
    )


def right_sides(real, imag, paired):
    zero = jnp.zeros_like(imag)
    turned = jnp.where(paired, zero, imag)
    upper = jnp.concatenate([real, turned], axis=1)
    lower = jnp.concatenate([-turned, jnp.where(paired, imag, real)], axis=1)
    return upper, lower


def own_kernel(paired_ref, weight_ref, x_ref, out_ref, held_ref, sems):
    cycle = weight_ref.shape[1]
    for copy in fetch(x_ref, held_ref, sems):
        copy.wait()
    upper, lower = right_sides(rows_of(held_ref, 0), rows_of(held_ref, 1), paired_ref[0] != 0)
    out_ref[...] = dot(weight_ref[0, :, :cycle], upper) + dot(weight_ref[1, :, :cycle], lower)


def back_sides(real, imag, paired):
    zero = jnp.zeros_like(imag)
    turned = jnp.where(paired, zero, imag)
    upper = jnp.concatenate([real, turned], axis=1)
    lower = jnp.concatenate([turned, jnp.where(paired, imag, -real)], axis=1)
    return upper, lower


def middle_kernel(paired_ref, own_ref, edge_ref, back_ref, near_ref, middle_ref, out_ref):
    paired = paired_ref[0] != 0
    width = near_ref.shape[2]
    upper, lower = right_sides(near_ref[0], near_ref[1], paired)
    middle = own_ref[...] + dot(edge_ref[0], upper) + dot(edge_ref[1], lower)
    middle = middle.astype(BF16)
    middle_ref[...] = middle
    upper, lower = back_sides(middle[:, :width], middle[:, width:], paired)
    out_ref[...] = (dot(back_ref[0], upper) + dot(back_ref[1], lower)).astype(BF16)


def back_kernel(paired_ref, turned_ref, middle_ref, out_ref):
    paired = paired_ref[0] != 0
    width = middle_ref.shape[1] // 2
    upper, lower = back_sides(middle_ref[:, :width], middle_ref[:, width:], paired)
    out_ref[...] = dot(turned_ref[0], upper) + dot(turned_ref[1], lower)


def finish_kernel(index_ref, back_ref, got_ref, out_ref):
    chunks, _, rows, width = out_ref.shape
    cycle = back_ref.shape[0]
    count = index_ref.shape[1]
    pick = lax.broadcasted_iota(jnp.int32, (cycle, count), 0) == index_ref[...]
    pick = jnp.where(pick, 1.0, 0.0).astype(BF16)
    total = (back_ref[...] + dot(pick, got_ref[...])).astype(BF16)
    for part in range(2):
        out_ref[:, part] = total[:, part * width : (part + 1) * width].reshape(chunks, rows, width)


def placed(operand, spec):
    space = spec.memory_space
    return pltpu.with_memory_space_constraint(operand, space) if space in (pltpu.VMEM, pltpu.HBM) else operand


def call(kernel, outs, specs, name, mebibytes, *operands, scratch=(), out_spaces=None):
    single = not isinstance(outs, (list, tuple))
    shapes = [outs] if single else list(outs)
    spaces = out_spaces or [pltpu.VMEM] * len(shapes)
    results = pl.pallas_call(
        kernel,
        out_shape=[space(out.shape, out.dtype) for out, space in zip(shapes, spaces)],
        in_specs=specs,
        out_specs=[pl.BlockSpec(memory_space=space) for space in spaces],
        scratch_shapes=scratch,
        compiler_params=pltpu.CompilerParams(vmem_limit_bytes=mebibytes * 1024 * 1024),
        name=name,
    )(*(placed(operand, spec) for operand, spec in zip(operands, specs)))
    return results[0] if single else list(results)


def per_device(loads, state, factors, assign, iface):
    local, cycle, width = loads.shape
    inner, outer = iface[0, 0], iface[0, 1]
    face = inner.shape[0]
    devices = lax.axis_size("sector")
    cycles = lax.axis_size("radial")
    here = lax.axis_index("radial")
    sectors = local * devices
    rows = cycle // devices
    aligned = rows % TILE == 0
    weight = factors[0]
    forward, inverse = tables(assign, sectors)
    paired = (assign[lax.axis_index("sector")] == 0).astype(jnp.int32).reshape(1)
    shape = jax.ShapeDtypeStruct

    def exchange(pieces):
        return lax.all_to_all(pieces, "sector", split_axis=0, concat_axis=0, tiled=True)

    def step(block, shift):
        pairs = [(i, i + shift) for i in range(cycles) if 0 <= i + shift < cycles]
        return lax.ppermute(block, "radial", pairs)

    if cycles == 2:
        toward = jnp.where(here == 0, outer, inner)
        away = jnp.where(here == 0, inner, outer)
        sent = jnp.concatenate([toward, away])
        gathered, scattered = toward, away
    else:
        sent = gathered = jnp.concatenate([inner, outer])
        scattered = jnp.concatenate([outer, inner])
    sent = sent.reshape(1, -1)
    scattered = scattered.reshape(1, -1)
    edges = gathered.shape[0]

    pieces = exchange(by_chunk(loads, devices)[0]).reshape(sectors, rows, width)

    edge, turned, outward = call(
        prepare_kernel,
        (shape((2, cycle, 2 * edges), BF16), shape((2, cycle, cycle), BF16), shape((2, edges, cycle), BF16)),
        [SMEM, VMEM, VMEM], "prepare", 20,
        (here == 0).astype(jnp.int32).reshape(1), gathered.reshape(1, -1), weight,
    )
    if aligned:
        wide = shape((sectors * TILE, sectors * TILE), BF16)
        forward, inverse = call(widen_kernel, (wide, wide), [VMEM, VMEM], "widen", 12, forward, inverse)
    state, token = by_chunk(state, devices)
    spectrum = transform(forward, pieces, token)
    harmonic = exchange(spectrum.reshape(devices, 2, rows, width))
    state = exchange(state).reshape(sectors, rows, width)
    if aligned:
        state = call(
            stage_kernel, shape(state.shape, BF16), [HBM], "stage", 8, state,
            scratch=(pltpu.SemaphoreType.DMA((4,)),),
        )

    if not aligned:
        harmonic = harmonic.transpose(1, 0, 2, 3).reshape(1, 2, cycle, width)
    faces = call(
        faces_kernel, shape((2, 2 * face, width), BF16), [VMEM, VMEM], "faces", 8, sent, harmonic,
    )
    own = call(
        own_kernel, shape((cycle, 2 * width), F32), [SMEM, VMEM, HBM], "own", 12, paired, weight, harmonic,
        scratch=fetch_scratch(harmonic),
    )
    if cycles == 2:
        near = lax.ppermute(faces, "radial", [(0, 1), (1, 0)])
    else:
        lower = step(faces, 1)
        upper = step(faces, -1)
        beyond_above = step(faces[:, :face], -2)
        beyond_below = step(faces[:, face:], 2)
        far_above = (upper[:, face:].astype(F32) + beyond_above.astype(F32)).astype(BF16)
        far_below = (lower[:, :face].astype(F32) + beyond_below.astype(F32)).astype(BF16)
        near = jnp.concatenate([lower[:, face:], upper[:, :face], far_above, far_below], axis=1)
    middle, leaving = call(
        middle_kernel,
        (shape((cycle, 2 * width), BF16), shape((edges, 2 * width), BF16)),
        [SMEM, VMEM, VMEM, VMEM, VMEM], "middle", 12,
        paired, own, edge, outward, near,
    )
    if cycles == 2:
        got = lax.ppermute(leaving, "radial", [(0, 1), (1, 0)])
    else:
        got = jnp.concatenate([step(leaving[:face], 1), step(leaving[face:], -1)], axis=0)
    back = call(
        back_kernel, shape((cycle, 2 * width), F32), [SMEM, VMEM, VMEM], "back", 12, paired, turned, middle
    )
    solved = call(
        finish_kernel, shape((devices, 2, rows, width) if aligned else (1, 2, cycle, width), BF16),
        [VMEM, VMEM, VMEM], "finish", 12, scattered, back, got,
    )
    if not aligned:
        solved = solved.reshape(2, devices, rows, width).transpose(1, 0, 2, 3)
    pieces = exchange(solved).reshape(sectors, rows, width)
    found = respond(inverse, pieces, state).reshape(devices, local, rows)
    return exchange(found).transpose(1, 0, 2).reshape(local, cycle)


def solution(mesh):
    return jax.shard_map(
        per_device,
        mesh=mesh,
        in_specs=(
            P("sector", "radial", None),
            P("sector", "radial", None),
            P("sector", None, "radial", None),
            P(),
            P("radial", None, None),
        ),
        out_specs=P("sector", "radial"),
        check_vma=False,
    )
```
